32 devices in a mesh: dp: 4 (over x, core), seq: 4 (over z), chan: 2 (over y).
Axes of the slice: x: 2, y: 2, z: 4, core: 2. Of those that a mesh axis runs over, the one named last changes fastest.
Arguments:
- inputs: bfloat16 [4, 8, 256, 2048], P('dp', 'seq', None, 'chan'), may hold values from -6 to 6
- cotangent: bfloat16 [4, 8, 256, 2048], P('dp', 'seq', None, 'chan'), may hold values from -6 to 6
- rows_in: bfloat16 [256, 256], replicated, may hold values from -0.375 to 0.375
- cols_mix: bfloat16 [8, 8], replicated, may hold values from -2 to 2
- blocks_gate: bfloat16 [4, 512, 512], P('chan'), may hold values from -0.25 to 0.25
- blocks_up: bfloat16 [4, 512, 512], P('chan'), may hold values from -0.25 to 0.25
- mix_gate: bfloat16 [4, 4, 512], replicated, may hold values from -3 to 3
- mix_up: bfloat16 [4, 4, 512], replicated, may hold values from -3 to 3
Outputs:
- input_grad: bfloat16 [4, 8, 256, 2048], P('dp', 'seq', None, 'chan')
- rows_grad: float32 [256, 256], replicated
- cols_grad: float32 [8, 8], replicated
- blocks_gate_grad: float32 [4, 512, 512], P('chan')
- blocks_up_grad: float32 [4, 512, 512], P('chan')
- mix_gate_grad: float32 [4, 4, 512], P(None, 'chan')
- mix_up_grad: float32 [4, 4, 512], P(None, 'chan')
The draws below stay inside these ranges and needn't reach their ends.
All inputs are finite; a program needn't handle non-finite values.
Results may differ from the reference program's by a relative error of at most 0.011.
Values may be sent and summed in bfloat16 or wider, within the bound.
No kernel may reach another device: no remote copies, remote signals or barrier semaphores. Data moves between devices by JAX's collectives and lax.ppermute only.
A program may use at most 128 MiB of HBM per device.

```python
import jax
import jax.numpy as jnp

D = 2048
NBLK = 4
BLK = 512
GC = 256
GR = 8
BATCH = 4


def steps_of(key, dims, pieces, smallest, largest):
    gain, own = 1.0, jax.random.fold_in(key, 6)
    for axis_at, parts in pieces:
        draws = jnp.exp(jax.random.uniform(jax.random.fold_in(own, axis_at), (parts,), jnp.float32, smallest / len(pieces), largest / len(pieces)))
        gain = gain * jnp.repeat(draws, dims[axis_at] // parts).reshape([-1 if axis == axis_at else 1 for axis in range(len(dims))])
    return gain


def noise(stream_key, dims, width, reach, cuts=(), held_as=jnp.bfloat16):
    factor_of = steps_of(stream_key, dims, cuts, -0.22, 0.18) if cuts else 1.0
    result = jax.random.normal(stream_key, dims, jnp.float32) * width * factor_of
    return jnp.minimum(jnp.maximum(result, -reach), reach).astype(held_as)


def setup_inputs(seed: int = 0) -> dict:
    key_list = jax.random.split(jax.random.key(seed), 9)
    return {
        "inputs": noise(key_list[0], (BATCH, GR, GC, D), 1.0, 6.0, ((0, 4), (1, 4), (3, 2))),
        "cotangent": noise(key_list[1], (BATCH, GR, GC, D), 1.0, 6.0, ((0, 4), (1, 4), (3, 2))),
        "rows_in": noise(key_list[2], (GC, GC), GC ** -0.5, 0.375),
        "cols_mix": noise(key_list[3], (GR, GR), GR ** -0.5, 2.0),
        "blocks_gate": noise(key_list[4], (NBLK, BLK, BLK), BLK ** -0.5, 0.25, ((0, 2),)),
        "blocks_up": noise(key_list[5], (NBLK, BLK, BLK), BLK ** -0.5, 0.25, ((0, 2),)),
        "mix_gate": noise(key_list[6], (NBLK, NBLK, BLK), NBLK ** -0.5, 3.0),
        "mix_up": noise(key_list[7], (NBLK, NBLK, BLK), NBLK ** -0.5, 3.0),
    }


def widen(value):
    return value.astype(jnp.float32)

def reference(inputs, cotangent, rows_in, cols_mix, blocks_gate, blocks_up, mix_gate, mix_up):
    split_shape = (BATCH, GR, GC, NBLK, BLK)
    first = jnp.einsum('ec,brcd->bred', widen(rows_in), widen(inputs)).astype(jnp.bfloat16)
    second = jnp.einsum('er,brcd->becd', widen(cols_mix), widen(first)).astype(jnp.bfloat16)
    hidden = (widen(inputs) + widen(second)).astype(jnp.bfloat16)
    hidden_blocks = widen(hidden).reshape(split_shape)
    gate_mid = jnp.einsum('brckj,kjl->brckl', hidden_blocks, widen(blocks_gate)).astype(jnp.bfloat16)
    up_mid = jnp.einsum('brckj,kjl->brckl', hidden_blocks, widen(blocks_up)).astype(jnp.bfloat16)
    gate_out = jnp.einsum('mkj,brckj->brcmj', widen(mix_gate), widen(gate_mid))
    up_out = jnp.einsum('mkj,brckj->brcmj', widen(mix_up), widen(up_mid))
    upstream = widen(cotangent).reshape(split_shape)
    sigma = jax.nn.sigmoid(gate_out)
    up_grad = (upstream * gate_out * sigma).astype(jnp.bfloat16)
    gate_grad = (upstream * up_out * sigma * (1.0 + gate_out * (1.0 - sigma))).astype(jnp.bfloat16)
    mix_gate_sum = jnp.einsum('brcmj,brckj->mkj', widen(gate_grad), widen(gate_mid))
    mix_up_sum = jnp.einsum('brcmj,brckj->mkj', widen(up_grad), widen(up_mid))
    gate_back = jnp.einsum('mkj,brcmj->brckj', widen(mix_gate), widen(gate_grad)).astype(jnp.bfloat16)
    up_back = jnp.einsum('mkj,brcmj->brckj', widen(mix_up), widen(up_grad)).astype(jnp.bfloat16)
    blocks_gate_sum = jnp.einsum('brckj,brckl->kjl', hidden_blocks, widen(gate_back))
    blocks_up_sum = jnp.einsum('brckj,brckl->kjl', hidden_blocks, widen(up_back))
    hidden_grad = upstream + jnp.einsum('brckl,kjl->brckj', widen(gate_back), widen(blocks_gate)) + jnp.einsum('brckl,kjl->brckj', widen(up_back), widen(blocks_up))
    hidden_grad = hidden_grad.reshape(BATCH, GR, GC, D).astype(jnp.bfloat16)
    cols_sum = jnp.einsum('becd,brcd->er', widen(hidden_grad), widen(first))
    first_grad = jnp.einsum('er,becd->brcd', widen(cols_mix), widen(hidden_grad)).astype(jnp.bfloat16)
    rows_sum = jnp.einsum('bred,brcd->ec', widen(first_grad), widen(inputs))
    input_grad = (widen(hidden_grad) + jnp.einsum('ec,bred->brcd', widen(rows_in), widen(first_grad))).astype(jnp.bfloat16)
    rows_scale = 1.0 / jnp.sqrt(jnp.float32(BATCH * GR * D))
    cols_scale = 1.0 / jnp.sqrt(jnp.float32(BATCH * GC * D))
    block_scale = 1.0 / jnp.sqrt(jnp.float32(BATCH * GR * GC))
    return (input_grad, rows_sum * rows_scale, cols_sum * cols_scale, blocks_gate_sum * block_scale, blocks_up_sum * block_scale, mix_gate_sum * block_scale, mix_up_sum * block_scale)
```

```python
import functools
import math

import jax
import jax.numpy as jnp
from jax import lax
from jax.experimental import pallas as pl
from jax.experimental.pallas import tpu as pltpu
from jax.sharding import PartitionSpec as P

BF = jnp.bfloat16
F = jnp.float32
VM = pl.BlockSpec(memory_space=pltpu.VMEM)
SM = pl.BlockSpec(memory_space=pltpu.SMEM)
PARAMS = pltpu.CompilerParams(vmem_limit_bytes=48 * 1024 * 1024)


def shape_of(dims, kind=BF):
    return jax.ShapeDtypeStruct(dims, kind)


def column_mix_kernel(n, rows, transpose, flat, place, mix, *refs):
    at = place[0]
    sources = refs[: n * rows] if flat else refs[:n]
    outs = refs[len(sources) :]
    width = outs[0].shape[-2]

    def chunk(t, carry):
        part = pl.ds(pl.multiple_of(t * 16, 16), 16)
        values = []
        for i in range(n):
            for h in range(rows):
                held = sources[i * rows + h][part, :] if flat else sources[i][h, part, :]
                values.append(held.astype(F))
        for i in range(n):
            for h in range(rows):
                e = lax.rem(at + i, n) * rows + h
                total = None
                for j in range(n):
                    for g in range(rows):
                        r = lax.rem(at + n - j, n) * rows + g
                        term = (mix[r, e] if transpose else mix[e, r]) * values[j * rows + g]
                        total = term if total is None else total + term
                if flat:
                    outs[i][h, part, :] = total.astype(BF)
                else:
                    outs[i * rows + h][part, :] = total.astype(BF)
        return carry

    lax.fori_loop(0, width // 16, chunk, 0)


def column_mix(place, mix, inputs, received):
    rows, cols, width = inputs.shape
    n = len(received) + 1
    cw = cols // n
    lanes = 256
    piece = pl.BlockSpec((rows, cw, lanes), lambda j, at: (0, 0, j))
    return pl.pallas_call(
        functools.partial(column_mix_kernel, n, rows, False, False),
        out_shape=[shape_of((cw, width))] * (n * rows),
        grid_spec=pltpu.PrefetchScalarGridSpec(
            num_scalar_prefetch=1,
            grid=(width // lanes,),
            in_specs=[SM, pl.BlockSpec((rows, cw, lanes), lambda j, at: (0, at[0], j))]
            + [piece] * (n - 1),
            out_specs=[pl.BlockSpec((cw, lanes), lambda j, at: (0, j))] * (n * rows),
        ),
        name="column_mix",
    )(place, mix, inputs, *received)


def column_back(place, mix, pieces, n, rows):
    cw, width = pieces[0].shape
    lanes = 256
    return pl.pallas_call(
        functools.partial(column_mix_kernel, n, rows, True, True),
        out_shape=[shape_of((rows, cw, width))] * n,
        grid_spec=pltpu.PrefetchScalarGridSpec(
            num_scalar_prefetch=1,
            grid=(width // lanes,),
            in_specs=[SM] + [pl.BlockSpec((cw, lanes), lambda j, at: (0, j))] * (n * rows),
            out_specs=[pl.BlockSpec((rows, cw, lanes), lambda j, at: (0, 0, j))] * n,
        ),
        name="column_back",
    )(place, mix, *pieces)


def column_sum_kernel(n, rows, place, x_own, *refs):
    at = place[0]
    received = refs[: n - 1]
    pieces = refs[n - 1 : n - 1 + n * rows]
    out, left, right = refs[n - 1 + n * rows :]
    cw = pieces[0].shape[0]
    for i in range(n):
        for h in range(rows):
            row = lax.rem(at + n - i, n) * rows + h
            spot = pl.ds(pl.multiple_of(row * cw, cw), cw)
            left[spot, :] = pieces[i * rows + h][...]
            right[spot, :] = x_own[h] if i == 0 else received[i - 1][h]
    product = lax.dot_general(
        left[...], right[...], (((1,), (1,)), ((), ())), preferred_element_type=F
    )
    size = n * rows * cw
    row_at = lax.broadcasted_iota(jnp.int32, (size, size), 0)
    col_at = lax.broadcasted_iota(jnp.int32, (size, size), 1)
    kept = jnp.where(lax.rem(row_at, cw) == lax.rem(col_at, cw), product, 0.0)
    out[...] = jnp.sum(kept.reshape(n * rows, cw, size), axis=1)


def column_sum(place, inputs, received, pieces):
    rows, cols, width = inputs.shape
    n = len(received) + 1
    cw = cols // n
    size = n * rows * cw
    whole = lambda *dims: pl.BlockSpec(dims, lambda j, at: (0,) * len(dims))
    return pl.pallas_call(
        functools.partial(column_sum_kernel, n, rows),
        out_shape=shape_of((n * rows, size), F),
        grid_spec=pltpu.PrefetchScalarGridSpec(
            num_scalar_prefetch=1,
            grid=(1,),
            in_specs=[pl.BlockSpec((rows, cw, width), lambda j, at: (0, at[0], 0))]
            + [whole(rows, cw, width)] * (n - 1)
            + [whole(cw, width)] * (n * rows),
            out_specs=whole(n * rows, size),
            scratch_shapes=[pltpu.VMEM((size, width), BF)] * 2,
        ),
        name="column_sum",
    )(place, inputs, *received, *pieces)


def hidden_kernel(n, place, rows_in, x, *refs):
    pieces = refs[:n]
    hidden, mixed = refs[n:]
    cw = pieces[0].shape[0]
    for i in range(n):
        spot = pl.multiple_of(lax.rem(place[0] + n - i, n) * cw, cw)
        mixed[pl.ds(spot, cw), :] = pieces[i][...]
    second = jnp.dot(rows_in[...], mixed[...], preferred_element_type=F)
    hidden[...] = (x[...].astype(F) + second).astype(BF)


def hidden_row(place, rows_in, inputs, h, pieces):
    cols, width = inputs.shape[1:]
    n = len(pieces)
    cw = cols // n
    lanes = 512
    column = pl.BlockSpec((cols, lanes), lambda j, at: (0, j))
    return pl.pallas_call(
        functools.partial(hidden_kernel, n),
        out_shape=[shape_of((cols, width))] * 2,
        grid_spec=pltpu.PrefetchScalarGridSpec(
            num_scalar_prefetch=1,
            grid=(width // lanes,),
            in_specs=[
                pl.BlockSpec((cols, cols), lambda j, at: (0, 0)),
                pl.BlockSpec((None, cols, lanes), lambda j, at: (h, 0, j)),
            ]
            + [pl.BlockSpec((cw, lanes), lambda j, at: (0, j))] * n,
            out_specs=[column, column],
        ),
        name="hidden_row",
    )(place, rows_in, inputs, *pieces)


def channel_kernel(n, place, *refs):
    (h_own, h_oth, c_own, c_oth, wg_own, wg_oth, wu_own, wu_oth, mix_g, mix_u, rows_in) = refs[:11]
    hid_grad, back_g, back_u, mix_sum = refs[11:15]
    pieces = refs[15 : 15 + n]
    mid_g, mid_u, turned = refs[15 + n :]
    local, size = wg_own.shape[:2]
    blocks = 2 * local
    cols = h_own.shape[0]
    for k in range(blocks):
        h, wg, wu = (h_own, wg_own, wu_own) if k < local else (h_oth, wg_oth, wu_oth)
        part = h[:, (k % local) * size : (k % local + 1) * size]
        mid_g[k] = jnp.dot(part, wg[k % local], preferred_element_type=F)
        mid_u[k] = jnp.dot(part, wu[k % local], preferred_element_type=F)
    mix_sum[...] = jnp.zeros_like(mix_sum)
    deep, lanes = 16, 128

    def chunk(t, carry):
        rows = pl.ds(pl.multiple_of(t * deep, deep), deep)
        for q in range(size // lanes):
            at = slice(q * lanes, (q + 1) * lanes)
            shape = (deep // 8, 8, lanes)
            g = [mid_g[k, rows, at].reshape(shape) for k in range(blocks)]
            u = [mid_u[k, rows, at].reshape(shape) for k in range(blocks)]
            sum_g, sum_u = [None] * local, [None] * local
            for m in range(blocks):
                c = c_own if m < local else c_oth
                start = (m % local) * size + q * lanes
                up = c[rows, start : start + lanes].astype(F).reshape(shape)
                gate_out = mix_g[m, 0, :, at] * g[0]
                up_out = mix_u[m, 0, :, at] * u[0]
                for k in range(1, blocks):
                    gate_out = gate_out + mix_g[m, k, :, at] * g[k]
                    up_out = up_out + mix_u[m, k, :, at] * u[k]
                sigma = 1.0 / (1.0 + jnp.exp(-gate_out))
                scaled = up * sigma
                up_grad = scaled * gate_out
                gate_grad = scaled * up_out * (1.0 + gate_out * (1.0 - sigma))
                for k in range(local):
                    mix_sum[0, m, k, :, at] += jnp.sum(gate_grad * g[k], axis=0)
                    mix_sum[1, m, k, :, at] += jnp.sum(up_grad * u[k], axis=0)
                    term_g = mix_g[m, k, :, at] * gate_grad
                    term_u = mix_u[m, k, :, at] * up_grad
                    sum_g[k] = term_g if m == 0 else sum_g[k] + term_g
                    sum_u[k] = term_u if m == 0 else sum_u[k] + term_u
            for k in range(local):
                spot = slice(k * size + q * lanes, k * size + (q + 1) * lanes)
                back_g[rows, spot] = sum_g[k].reshape(deep, lanes).astype(BF)
                back_u[rows, spot] = sum_u[k].reshape(deep, lanes).astype(BF)
        return carry

    lax.fori_loop(0, cols // deep, chunk, 0)
    last = (((1,), (1,)), ((), ()))
    for k in range(local):
        spot = slice(k * size, (k + 1) * size)
        grad = lax.dot_general(back_g[:, spot], wg_own[k], last, preferred_element_type=F)
        grad = grad + lax.dot_general(back_u[:, spot], wu_own[k], last, preferred_element_type=F)
        hid_grad[:, spot] = (c_own[:, spot].astype(F) + grad).astype(BF)
    turned[...] = lax.dot_general(
        rows_in[...], hid_grad[...], (((0,), (0,)), ((), ())), preferred_element_type=F
    ).astype(BF)
    cw = cols // n
    for i in range(n):
        spot = pl.multiple_of(lax.rem(place[0] + i, n) * cw, cw)
        pieces[i][...] = turned[pl.ds(spot, cw), :]


def channel_row(n, place, h, h_own, h_oth, cot, cot_oth, weights, mixes, rows_in):
    cols, width = h_own.shape
    local, size = weights[0].shape[:2]
    blocks = 2 * local
    whole = lambda *dims: pl.BlockSpec(dims, lambda j, at: (0,) * len(dims))
    row = pl.BlockSpec((None, cols, width), lambda j, at: (h, 0, 0))
    cw = cols // n
    return pl.pallas_call(
        functools.partial(channel_kernel, n),
        out_shape=[shape_of((cols, width))] * 3
        + [shape_of((2, blocks, local, 8, size), F)]
        + [shape_of((cw, width))] * n,
        grid_spec=pltpu.PrefetchScalarGridSpec(
            num_scalar_prefetch=1,
            grid=(1,),
            in_specs=[whole(cols, width)] * 2
            + [row, row]
            + [whole(local, size, size)] * 4
            + [whole(blocks, blocks, 8, size)] * 2
            + [whole(cols, cols)],
            out_specs=[whole(cols, width)] * 3
            + [whole(2, blocks, local, 8, size)]
            + [whole(cw, width)] * n,
            scratch_shapes=[pltpu.VMEM((blocks, cols, size), F)] * 2
            + [pltpu.VMEM((cols, width), BF)],
        ),
        compiler_params=PARAMS,
        name="channel_row",
    )(place, h_own, h_oth, cot, cot_oth, *weights, *mixes, rows_in)


def sums_kernel(rows, parts, place, *refs):
    hid, back_g, back_u, grad, mixed, mix_sum = (refs[i * rows : (i + 1) * rows] for i in range(6))
    out, row_sum = refs[6 * rows :]
    cols, width = hid[0].shape
    size = out.shape[-1]
    local = width // size
    blocks = 2 * local
    first = (((0,), (0,)), ((), ()))
    last = (((1,), (1,)), ((), ()))
    high = local * size // parts
    per = size // high
    for w, back in enumerate((back_g, back_u)):
        for k in range(local):
            spot = slice(k * size, (k + 1) * size)
            total = None
            for h in range(rows):
                term = lax.dot_general(
                    hid[h][:, spot], back[h][:, spot], first, preferred_element_type=F
                )
                total = term if total is None else total + term
            for q in range(per):
                out[k * per + q, w * high : (w + 1) * high, :] = total[
                    q * high : (q + 1) * high
                ].astype(BF)
    total = None
    for h in range(rows):
        term = lax.dot_general(grad[h][...], mixed[h][...], last, preferred_element_type=F)
        total = term if total is None else total + term
    row_sum[...] = total
    chan = place[1]
    for p in range(parts):
        w, m, k = p // (blocks * local), (p // local) % blocks, p % local
        m_at = lax.rem(m + blocks - chan * local, blocks)
        held = sum(ref[w, m_at, k] for ref in mix_sum)
        line = jnp.broadcast_to(jnp.sum(held, axis=0, keepdims=True), (8, size))
        eight = jnp.concatenate(
            [row_sum[16 * p : 16 * p + 8, :], row_sum[16 * p + 8 : 16 * p + 16, :]], axis=1
        )
        out[p, 2 * high :, :] = jnp.concatenate([eight, line], axis=0).astype(BF)


def sums(place, parts, hid, back_g, back_u, grad, mixed, mix_sum):
    rows = len(hid)
    cols = hid[0].shape[0]
    size = mix_sum[0].shape[-1]
    high = hid[0].shape[1] // parts
    return pl.pallas_call(
        functools.partial(sums_kernel, rows, parts),
        out_shape=shape_of((parts, 2 * high + 16, size)),
        in_specs=[SM] + [VM] * (6 * rows),
        out_specs=VM,
        scratch_shapes=[pltpu.VMEM((cols, cols), F)],
        compiler_params=PARAMS,
        name="sums",
    )(place, *hid, *back_g, *back_u, *grad, *mixed, *mix_sum)


def unpack_kernel(n, scales, place, *refs):
    held = refs[:4]
    gate, up, rows, mix = refs[4:]
    at, core, x = place[0], place[2], place[3]
    high = gate.shape[0] // (4 * n)
    half = rows.shape[1]
    for i in range(4):
        base = lax.rem(core + i // 2, 2) * 2 * n + lax.rem(x + i % 2, 2) * n
        for j in range(n):
            p = base + lax.rem(at + n - j, n)
            spot = pl.ds(pl.multiple_of(p * high, high), high)
            gate[spot, :] = held[i][j, :high, :].astype(F) * scales[1]
            up[spot, :] = held[i][j, high : 2 * high, :].astype(F) * scales[1]
            tail = held[i][j, 2 * high :, :].astype(F)
            where = pl.multiple_of(p * 16, 16)
            rows[pl.ds(where, 8), :] = tail[:8, :half] * scales[0]
            rows[pl.ds(where + 8, 8), :] = tail[:8, half:] * scales[0]
            mix[pl.ds(p, 1), :] = tail[8:9, :] * scales[1]


def unpack(n, scales, place, held, cols):
    deep, size = held[0].shape[1:]
    high = (deep - 16) // 2
    return pl.pallas_call(
        functools.partial(unpack_kernel, n, scales),
        out_shape=[shape_of((4 * n * high, size), F)] * 2
        + [shape_of((cols, cols), F), shape_of((4 * n, size), F)],
        in_specs=[SM] + [VM] * 4,
        out_specs=[VM] * 4,
        compiler_params=PARAMS,
        name="unpack",
    )(place, *held)


def finish_kernel(n, place, *refs):
    grads, pieces, out = refs[:-1 - n], refs[-1 - n : -1], refs[-1]
    cw = pieces[0].shape[1]
    for i in range(n):
        spot = pl.ds(pl.multiple_of(lax.rem(place[0] + n - i, n) * cw, cw), cw)
        for h, grad in enumerate(grads):
            out[h, spot, :] = (grad[spot, :].astype(F) + pieces[i][h].astype(F)).astype(BF)


def finish(place, grads, pieces):
    cols, width = grads[0].shape
    rows, cw = pieces[0].shape[:2]
    n = len(pieces)
    lanes = 512
    return pl.pallas_call(
        functools.partial(finish_kernel, n),
        out_shape=shape_of((rows, cols, width)),
        grid=(width // lanes,),
        in_specs=[SM]
        + [pl.BlockSpec((cols, lanes), lambda j: (0, j))] * rows
        + [pl.BlockSpec((rows, cw, lanes), lambda j: (0, 0, j))] * n,
        out_specs=pl.BlockSpec((rows, cols, lanes), lambda j: (0, 0, j)),
        name="finish",
    )(place, *grads, *pieces)


def shifted(value, by, n):
    return lax.ppermute(value, "seq", [(i, (i + by) % n) for i in range(n)])


def swapped(value, axis, bit, n):
    return lax.ppermute(value, axis, [(i, i ^ bit) for i in range(n)])


def pick(value, index):
    return lax.dynamic_index_in_dim(value, index, 0, keepdims=False)


def add(*values):
    return sum(value.astype(F) for value in values).astype(BF)


def reduce_parts(packed, seq_at, core, x, n):
    deep, size = packed.shape[1:]
    halves = packed.reshape(2, 2 * n, deep, size)
    got = swapped(pick(halves, 1 - core), "dp", 1, 4)
    halves = add(pick(halves, core), got).reshape(2, n, deep, size)
    got = swapped(pick(halves, 1 - x), "dp", 2, 4)
    fours = add(pick(halves, x), got)
    got = [shifted(pick(fours, lax.rem(seq_at + i, n)), i, n) for i in range(1, n)]
    mine = add(pick(fours, seq_at), *got)
    tail = mine[deep - 16 :]
    other = swapped(tail, "chan", 1, 2)
    is_rows = lax.broadcasted_iota(jnp.int32, tail.shape, 0) < 8
    tail = jnp.where(is_rows, add(tail, other), tail)
    mine = jnp.concatenate([mine[: deep - 16], tail], axis=0)
    held = jnp.stack([mine] + [shifted(mine, i, n) for i in range(1, n)])
    by_x = swapped(held, "dp", 2, 4)
    return held, by_x, swapped(held, "dp", 1, 4), swapped(by_x, "dp", 1, 4)


def block_body(inputs, cotangent, rows_in, cols_mix, blocks_gate, blocks_up, mix_gate, mix_up):
    n = lax.axis_size("seq")
    rows, cols, width = inputs.shape[1:]
    local, size = blocks_gate.shape[:2]
    cw = cols // n
    seq_at, chan_at, dp_at = lax.axis_index("seq"), lax.axis_index("chan"), lax.axis_index("dp")
    core, x = lax.rem(dp_at, 2), dp_at // 2
    place = jnp.stack([seq_at, chan_at, core, x]).astype(jnp.int32)
    values, cot = inputs[0], cotangent[0]
    mix = cols_mix.astype(F)

    def relative(table):
        turned = jnp.roll(table, (local, local), (0, 1))
        table = jnp.where(chan_at == 0, table, turned).astype(F)
        return jnp.broadcast_to(table[:, :, None, :], table.shape[:2] + (8, size))

    sent = [
        lax.dynamic_slice_in_dim(values, lax.rem(seq_at + i, n) * cw, cw, 1) for i in range(1, n)
    ]
    received = [shifted(sent[i - 1], i, n) for i in range(1, n)]
    cot_oth = swapped(cot, "chan", 1, 2)
    lent = swapped(jnp.where(core == 0, blocks_gate, blocks_up), "chan", 1, 2)
    lent_too = swapped(lent, "dp", 1, 4)
    gate_oth = jnp.where(core == 0, lent, lent_too)
    up_oth = jnp.where(core == 0, lent_too, lent)
    weights = (blocks_gate, gate_oth, blocks_up, up_oth)
    mixes = (relative(mix_gate), relative(mix_up))

    mixed_cols = column_mix(place, mix, values, received)
    pieces = [
        [mixed_cols[h]] + [shifted(mixed_cols[i * rows + h], i, n) for i in range(1, n)]
        for h in range(rows)
    ]
    hidden, mixed, grads, back_g, back_u, mix_sum, sources = [], [], [], [], [], [], []
    for h in range(rows):
        hid, mi = hidden_row(place, rows_in, values, h, pieces[h])
        hid_oth = swapped(hid, "chan", 1, 2)
        got = channel_row(n, place, h, hid, hid_oth, cot, cot_oth, weights, mixes, rows_in)
        hidden.append(hid)
        mixed.append(mi)
        grads.append(got[0])
        back_g.append(got[1])
        back_u.append(got[2])
        mix_sum.append(got[3])
        sources.append([got[4]] + [shifted(got[4 + i], i, n) for i in range(1, n)])
    packed = sums(place, 4 * n, hidden, back_g, back_u, grads, mixed, mix_sum)
    flat = [sources[h][i] for i in range(n) for h in range(rows)]
    back = column_back(place, mix, flat, n, rows)
    back = [back[0]] + [shifted(back[i], i, n) for i in range(1, n)]
    cols_sum = column_sum(place, values, received, flat)
    cols_sum = cols_sum.reshape(n * rows, n * rows, cw).sum(-1)
    for axis, bit, count in (("dp", 1, 4), ("dp", 2, 4), ("chan", 1, 2), ("seq", 1, n), ("seq", 2, n)):
        cols_sum = cols_sum + swapped(cols_sum, axis, bit, count)
    batch_all = lax.axis_size("dp")
    width_all = width * lax.axis_size("chan")
    rows_scale = 1.0 / math.sqrt(batch_all * rows * n * width_all)
    cols_scale = 1.0 / math.sqrt(batch_all * cols * width_all)
    block_scale = 1.0 / math.sqrt(batch_all * rows * n * cols)
    held = reduce_parts(packed, seq_at, core, x, n)
    gate_sum, up_sum, rows_sum, mix_out = unpack(n, (rows_scale, block_scale), place, held, cols)
    input_grad = finish(place, grads, back)
    mix_out = mix_out.reshape(2, 2 * local, local, size)
    return (
        input_grad[None],
        rows_sum,
        cols_sum * cols_scale,
        gate_sum.reshape(local, size, size),
        up_sum.reshape(local, size, size),
        mix_out[0],
        mix_out[1],
    )


def column_keep(segment, cols_mix):
    mixed = jnp.einsum(
        "er,brcd->becd", cols_mix, segment, preferred_element_type=jnp.float32
    ).astype(jnp.bfloat16)
    return (segment, mixed)

def body(inputs, cotangent, rows_in, cols_mix, blocks_gate, blocks_up, mix_gate, mix_up):
    batch_dev, rows_dev, cols_all, width_dev = inputs.shape
    block_size = blocks_gate.shape[1]
    local_blocks = blocks_gate.shape[0]
    chan_index = lax.axis_index("chan")
    split_shape = (batch_dev, rows_dev, cols_all, local_blocks, block_size)
    first = jnp.einsum("ec,brcd->bred", rows_in, inputs, preferred_element_type=jnp.float32).astype(
        jnp.bfloat16
    )
    first_cols, second_cols = column_keep(
        lax.all_to_all(first, "seq", split_axis=2, concat_axis=1, tiled=True), cols_mix
    )
    second_rows = lax.all_to_all(second_cols, "seq", split_axis=1, concat_axis=2, tiled=True)
    hidden = (inputs.astype(jnp.float32) + second_rows.astype(jnp.float32)).astype(jnp.bfloat16)
    hidden_blocks = hidden.reshape(split_shape)
    gate_rows_own = lax.dynamic_slice_in_dim(
        mix_gate, chan_index * local_blocks, local_blocks, 0
    ).astype(jnp.float32)
    up_rows_own = lax.dynamic_slice_in_dim(
        mix_up, chan_index * local_blocks, local_blocks, 0
    ).astype(jnp.float32)
    gate_mid = jnp.einsum(
        "brckj,kjl->brckl", hidden_blocks, blocks_gate, preferred_element_type=jnp.float32
    ).astype(jnp.bfloat16)
    up_mid = jnp.einsum(
        "brckj,kjl->brckl", hidden_blocks, blocks_up, preferred_element_type=jnp.float32
    ).astype(jnp.bfloat16)
    gate_add = jnp.einsum(
        "mkj,brckj->brcmj",
        gate_rows_own,
        lax.all_gather(gate_mid, "chan", axis=3, tiled=True).astype(jnp.float32),
    )
    up_add = jnp.einsum(
        "mkj,brckj->brcmj",
        up_rows_own,
        lax.all_gather(up_mid, "chan", axis=3, tiled=True).astype(jnp.float32),
    )
    upstream = cotangent.astype(jnp.float32).reshape(split_shape)
    sigma = jax.nn.sigmoid(gate_add)
    up_grad = (upstream * gate_add * sigma).astype(jnp.bfloat16)
    gate_grad = (upstream * up_add * sigma * (1.0 + gate_add * (1.0 - sigma))).astype(jnp.bfloat16)
    gate_all, up_all = (
        lax.all_gather(gate_grad, "chan", axis=3, tiled=True),
        lax.all_gather(up_grad, "chan", axis=3, tiled=True),
    )
    gate_cols_own = lax.dynamic_slice_in_dim(
        mix_gate, chan_index * local_blocks, local_blocks, 1
    ).astype(jnp.float32)
    up_cols_own = lax.dynamic_slice_in_dim(
        mix_up, chan_index * local_blocks, local_blocks, 1
    ).astype(jnp.float32)
    mix_gate_sum = jnp.einsum(
        "brcmj,brckj->mkj", gate_all, gate_mid, preferred_element_type=jnp.float32
    )
    mix_up_sum = jnp.einsum("brcmj,brckj->mkj", up_all, up_mid, preferred_element_type=jnp.float32)
    gate_back = jnp.einsum("mkj,brcmj->brckj", gate_cols_own, gate_all.astype(jnp.float32)).astype(
        jnp.bfloat16
    )
    up_back = jnp.einsum("mkj,brcmj->brckj", up_cols_own, up_all.astype(jnp.float32)).astype(
        jnp.bfloat16
    )
    blocks_gate_sum = jnp.einsum(
        "brckj,brckl->kjl", hidden_blocks, gate_back, preferred_element_type=jnp.float32
    )
    blocks_up_sum = jnp.einsum(
        "brckj,brckl->kjl", hidden_blocks, up_back, preferred_element_type=jnp.float32
    )
    hidden_grad = (
        upstream
        + jnp.einsum("brckl,kjl->brckj", gate_back, blocks_gate, preferred_element_type=jnp.float32)
        + jnp.einsum("brckl,kjl->brckj", up_back, blocks_up, preferred_element_type=jnp.float32)
    )
    hidden_grad = hidden_grad.reshape(inputs.shape).astype(jnp.bfloat16)
    segment = lax.all_to_all(hidden_grad, "seq", split_axis=2, concat_axis=1, tiled=True)
    mixed = jnp.einsum(
        "er,becd->brcd", cols_mix, segment, preferred_element_type=jnp.float32
    ).astype(jnp.bfloat16)
    cols_sum = jnp.einsum("becd,brcd->er", segment, first_cols, preferred_element_type=jnp.float32)
    first_grad = lax.all_to_all(mixed, "seq", split_axis=1, concat_axis=2, tiled=True)
    rows_sum = jnp.einsum("bred,brcd->ec", first_grad, inputs, preferred_element_type=jnp.float32)
    input_grad = (
        hidden_grad.astype(jnp.float32)
        + jnp.einsum("ec,bred->brcd", rows_in, first_grad, preferred_element_type=jnp.float32)
    ).astype(jnp.bfloat16)
    rows_total, cols_total = lax.psum((rows_sum, cols_sum), ("dp", "seq", "chan"))
    gate_blocks_total, up_blocks_total, gate_mix_total, up_mix_total = lax.psum(
        (blocks_gate_sum, blocks_up_sum, mix_gate_sum, mix_up_sum), ("dp", "seq")
    )
    count_dp = lax.axis_size("dp")
    count_seq = lax.axis_size("seq")
    count_chan = lax.axis_size("chan")
    batch_all = batch_dev * count_dp
    rows_all = rows_dev * count_seq
    width_all = width_dev * count_chan
    rows_scale = 1.0 / math.sqrt(batch_all * rows_all * width_all)
    cols_scale = 1.0 / math.sqrt(batch_all * cols_all * width_all)
    block_scale = 1.0 / math.sqrt(batch_all * rows_all * cols_all)
    return (
        input_grad,
        rows_total * rows_scale,
        cols_total * cols_scale,
        gate_blocks_total * block_scale,
        up_blocks_total * block_scale,
        gate_mix_total * block_scale,
        up_mix_total * block_scale,
    )


def solution(mesh):
    in_specs = (
        P("dp", "seq", None, "chan"),
        P("dp", "seq", None, "chan"),
        P(),
        P(),
        P("chan", None, None),
        P("chan", None, None),
        P(),
        P(),
    )
    out_specs = (
        P("dp", "seq", None, "chan"),
        P(),
        P(),
        P("chan", None, None),
        P("chan", None, None),
        P(None, "chan", None),
        P(None, "chan", None),
    )
    sizes = dict(mesh.shape)
    fits = sizes["dp"] == 4 and sizes["seq"] == 4 and sizes["chan"] == 2
    return jax.shard_map(block_body if fits else body, mesh=mesh, in_specs=in_specs, out_specs=out_specs, check_vma=False)
```

```python
import functools
import math

import jax
import jax.numpy as jnp
from jax import lax
from jax.experimental import pallas as pl
from jax.experimental.pallas import tpu as pltpu
from jax.sharding import PartitionSpec as P

BF = jnp.bfloat16
F = jnp.float32
VM = pl.BlockSpec(memory_space=pltpu.VMEM)
SM = pl.BlockSpec(memory_space=pltpu.SMEM)
PARAMS = pltpu.CompilerParams(vmem_limit_bytes=48 * 1024 * 1024)


def shape_of(dims, kind=BF):
    return jax.ShapeDtypeStruct(dims, kind)


def mix_tables(mix, rows, cw):
    size = mix.shape[0] * cw
    same = lax.broadcasted_iota(jnp.int32, (1, cw, 1, cw), 1) == lax.broadcasted_iota(
        jnp.int32, (1, cw, 1, cw), 3
    )

    def spread(table):
        grown = jnp.where(same, table[:, None, :, None], jnp.zeros((), BF))
        return grown.reshape(table.shape[0] * cw, table.shape[1] * cw)

    ahead = jnp.stack([spread(mix[h::rows]) for h in range(rows)])
    back = jnp.stack([spread(mix[h::rows].T) for h in range(rows)])
    assert ahead.shape[2] == back.shape[1] == size
    return ahead, back


def column_mix_kernel(rows, table, x_cols, *outs):
    for h in range(rows):
        outs[h][...] = jnp.dot(table[h], x_cols[...], preferred_element_type=F).astype(BF)


def column_mix(table, x_cols):
    rows, deep, size = table.shape
    width = x_cols.shape[-1]
    lanes = 512
    return pl.pallas_call(
        functools.partial(column_mix_kernel, rows),
        out_shape=[shape_of((deep, width))] * rows,
        grid=(width // lanes,),
        in_specs=[
            pl.BlockSpec((rows, deep, size), lambda j: (0, 0, 0)),
            pl.BlockSpec((size, lanes), lambda j: (0, j)),
        ],
        out_specs=[pl.BlockSpec((deep, lanes), lambda j: (0, j))] * rows,
        name="column_mix",
    )(table, x_cols)


def column_back_kernel(rows, table, *refs):
    total = None
    for h in range(rows):
        term = jnp.dot(table[h], refs[h][...], preferred_element_type=F)
        total = term if total is None else total + term
    refs[rows][...] = total.astype(BF)


def column_back(table, pieces):
    rows, size, deep = table.shape
    width = pieces[0].shape[-1]
    lanes = 512
    return pl.pallas_call(
        functools.partial(column_back_kernel, rows),
        out_shape=shape_of((size, width)),
        grid=(width // lanes,),
        in_specs=[pl.BlockSpec((rows, size, deep), lambda j: (0, 0, 0))]
        + [pl.BlockSpec((deep, lanes), lambda j: (0, j))] * rows,
        out_specs=pl.BlockSpec((size, lanes), lambda j: (0, j)),
        name="column_back",
    )(table, *pieces)


def column_sum_kernel(rows, x_cols, *refs):
    pieces, (out, left) = refs[:rows], refs[rows:]
    n, cw, width = pieces[0].shape
    for i in range(n):
        for h in range(rows):
            row = i * rows + h
            left[row * cw : (row + 1) * cw, :] = pieces[h][i]
    size = n * rows * cw
    product = lax.dot_general(
        left[...],
        x_cols[...].reshape(size, width),
        (((1,), (1,)), ((), ())),
        preferred_element_type=F,
    )
    row_at = lax.broadcasted_iota(jnp.int32, (size, size), 0)
    col_at = lax.broadcasted_iota(jnp.int32, (size, size), 1)
    kept = jnp.where(lax.rem(row_at, cw) == lax.rem(col_at, cw), product, 0.0)
    out[...] = jnp.sum(kept.reshape(n * rows, cw, size), axis=1)


def column_sum(x_cols, pieces):
    n, rows, cw, width = x_cols.shape
    size = n * rows * cw
    return pl.pallas_call(
        functools.partial(column_sum_kernel, rows),
        out_shape=shape_of((n * rows, size), F),
        in_specs=[VM] * (1 + rows),
        out_specs=VM,
        scratch_shapes=[pltpu.VMEM((size, width), BF)],
        compiler_params=PARAMS,
        name="column_sum",
    )(x_cols, *pieces)


def hidden_kernel(rows_in, x, mixed, hidden):
    second = jnp.dot(rows_in[...], mixed[...], preferred_element_type=F)
    hidden[...] = (x[...].astype(F) + second).astype(BF)


def hidden_row(rows_in, inputs, h, mixed):
    cols, width = mixed.shape
    lanes = 512
    column = pl.BlockSpec((cols, lanes), lambda j: (0, j))
    return pl.pallas_call(
        hidden_kernel,
        out_shape=shape_of((cols, width)),
        grid=(width // lanes,),
        in_specs=[
            pl.BlockSpec((cols, cols), lambda j: (0, 0)),
            pl.BlockSpec((None, cols, lanes), lambda j: (h, 0, j)),
            column,
        ],
        out_specs=column,
        name="hidden_row",
    )(rows_in, inputs, mixed)


def channel_kernel(*refs):
    (h_own, h_oth, c_own, c_oth, wg_own, wg_oth, wu_own, wu_oth, mix_g, mix_u, rows_in) = refs[:11]
    hid_grad, back_g, back_u, turned, mix_sum, mid_g, mid_u = refs[11:]
    local, size = wg_own.shape[:2]
    blocks = 2 * local
    cols = h_own.shape[0]
    for k in range(blocks):
        h, wg, wu = (h_own, wg_own, wu_own) if k < local else (h_oth, wg_oth, wu_oth)
        part = h[:, (k % local) * size : (k % local + 1) * size]
        mid_g[k] = jnp.dot(part, wg[k % local], preferred_element_type=F)
        mid_u[k] = jnp.dot(part, wu[k % local], preferred_element_type=F)
    mix_sum[...] = jnp.zeros_like(mix_sum)
    deep, lanes = 16, 128

    def chunk(t, carry):
        rows = pl.ds(pl.multiple_of(t * deep, deep), deep)
        for q in range(size // lanes):
            at = slice(q * lanes, (q + 1) * lanes)
            shape = (deep // 8, 8, lanes)
            g = [mid_g[k, rows, at].reshape(shape) for k in range(blocks)]
            u = [mid_u[k, rows, at].reshape(shape) for k in range(blocks)]
            sum_g, sum_u = [None] * local, [None] * local
            for m in range(blocks):
                c = c_own if m < local else c_oth
                start = (m % local) * size + q * lanes
                up = c[rows, start : start + lanes].astype(F).reshape(shape)
                gate_out = mix_g[m, 0, :, at] * g[0]
                up_out = mix_u[m, 0, :, at] * u[0]
                for k in range(1, blocks):
                    gate_out = gate_out + mix_g[m, k, :, at] * g[k]
                    up_out = up_out + mix_u[m, k, :, at] * u[k]
                sigma = 0.5 * jnp.tanh(0.5 * gate_out) + 0.5
                scaled = up * sigma
                up_grad = scaled * gate_out
                gate_grad = scaled * up_out * (1.0 + gate_out * (1.0 - sigma))
                for k in range(local):
                    mix_sum[0, m, k, :, at] += jnp.sum(gate_grad * g[k], axis=0)
                    mix_sum[1, m, k, :, at] += jnp.sum(up_grad * u[k], axis=0)
                    term_g = mix_g[m, k, :, at] * gate_grad
                    term_u = mix_u[m, k, :, at] * up_grad
                    sum_g[k] = term_g if m == 0 else sum_g[k] + term_g
                    sum_u[k] = term_u if m == 0 else sum_u[k] + term_u
            for k in range(local):
                spot = slice(k * size + q * lanes, k * size + (q + 1) * lanes)
                back_g[rows, spot] = sum_g[k].reshape(deep, lanes).astype(BF)
                back_u[rows, spot] = sum_u[k].reshape(deep, lanes).astype(BF)
        return carry

    lax.fori_loop(0, cols // deep, chunk, 0)
    last = (((1,), (1,)), ((), ()))
    for k in range(local):
        spot = slice(k * size, (k + 1) * size)
        grad = lax.dot_general(back_g[:, spot], wg_own[k], last, preferred_element_type=F)
        grad = grad + lax.dot_general(back_u[:, spot], wu_own[k], last, preferred_element_type=F)
        hid_grad[:, spot] = (c_own[:, spot].astype(F) + grad).astype(BF)
    turned[...] = lax.dot_general(
        rows_in[...], hid_grad[...], (((0,), (0,)), ((), ())), preferred_element_type=F
    ).astype(BF)


def channel_row(h, h_own, h_oth, cot, cot_oth, weights, mixes, rows_in):
    cols, width = h_own.shape
    local, size = weights[0].shape[:2]
    blocks = 2 * local
    row = pl.BlockSpec((None, cols, width), lambda j: (h, 0, 0))
    return pl.pallas_call(
        channel_kernel,
        out_shape=[shape_of((cols, width))] * 4 + [shape_of((2, blocks, local, 8, size), F)],
        grid=(1,),
        in_specs=[VM] * 2 + [row, row] + [VM] * 7,
        out_specs=[VM] * 5,
        scratch_shapes=[pltpu.VMEM((blocks, cols, size), F)] * 2,
        compiler_params=PARAMS,
        name="channel_row",
    )(h_own, h_oth, cot, cot_oth, *weights, *mixes, rows_in)


def sums_kernel(rows, parts, place, *refs):
    hid, back_g, back_u, grad, mixed, mix_sum = (refs[i * rows : (i + 1) * rows] for i in range(6))
    outs, row_sum = refs[6 * rows : -1], refs[-1]
    cols, width = hid[0].shape
    size = outs[0].shape[-1]
    local = width // size
    blocks = 2 * local
    first = (((0,), (0,)), ((), ()))
    last = (((1,), (1,)), ((), ()))
    high = local * size // parts
    per = size // high
    total = None
    for h in range(rows):
        term = lax.dot_general(grad[h][...], mixed[h][...], last, preferred_element_type=F)
        total = term if total is None else total + term
    row_sum[...] = total
    chan, core = place[1], place[2]
    for part, out in ((1, outs[1]), (0, outs[0])):
        k = core if part == 0 else 1 - core
        spot = pl.ds(pl.multiple_of(k * size, size), size)
        for w, back in enumerate((back_g, back_u)):
            total = None
            for h in range(rows):
                term = lax.dot_general(
                    hid[h][:, spot], back[h][:, spot], first, preferred_element_type=F
                )
                total = term if total is None else total + term
            for q in range(per):
                out[q, w * high : (w + 1) * high, :] = total[q * high : (q + 1) * high].astype(BF)
        for q in range(per):
            p = k * per + q
            m_at = lax.rem(p // (2 * local) + blocks - chan * local, blocks)
            k_at = lax.rem(p // 2, local)
            lines = [
                jnp.sum(sum(ref[w, m_at, k_at] for ref in mix_sum), axis=0, keepdims=True)
                for w in range(2)
            ]
            at = pl.multiple_of(p * 16, 16)
            eight = jnp.concatenate(
                [row_sum[pl.ds(at, 8), :], row_sum[pl.ds(at + 8, 8), :]], axis=1
            )
            blank = jnp.zeros((6, size), F)
            out[q, 2 * high :, :] = jnp.concatenate([eight, *lines, blank], axis=0).astype(BF)


def sums(place, parts, hid, back_g, back_u, grad, mixed, mix_sum):
    rows = len(hid)
    cols = hid[0].shape[0]
    size = mix_sum[0].shape[-1]
    high = hid[0].shape[1] // parts
    return pl.pallas_call(
        functools.partial(sums_kernel, rows, parts),
        out_shape=[shape_of((parts // 2, 2 * high + 16, size))] * 2,
        in_specs=[SM] + [VM] * (6 * rows),
        out_specs=[VM] * 2,
        scratch_shapes=[pltpu.VMEM((cols, cols), F)],
        compiler_params=PARAMS,
        name="sums",
    )(place, *hid, *back_g, *back_u, *grad, *mixed, *mix_sum)


def unpack_kernel(n, scales, place, *refs):
    held = refs[:4]
    gate, up, rows, mix_g, mix_u, cols_out, lines = refs[4:]
    local = mix_g.shape[1]
    at, core, x = place[0], place[2], place[3]
    high = gate.shape[0] // (4 * n)
    half = rows.shape[1]
    for i in range(4):
        base = lax.rem(core + i // 2, 2) * 2 * n + lax.rem(x + i % 2, 2) * n
        for j in range(n):
            p = base + lax.rem(at + n - j, n)
            spot = pl.ds(pl.multiple_of(p * high, high), high)
            gate[spot, :] = held[i][j, :high, :].astype(F) * scales[1]
            up[spot, :] = held[i][j, high : 2 * high, :].astype(F) * scales[1]
            tail = held[i][j, 2 * high :, :].astype(F)
            where = pl.multiple_of(p * 16, 16)
            rows[pl.ds(where, 8), :] = tail[:8, :half] * scales[0]
            rows[pl.ds(where + 8, 8), :] = tail[:8, half:] * scales[0]
            for w, out in enumerate((mix_g, mix_u)):
                spot = (pl.ds(p // (2 * local), 1), pl.ds(lax.rem(p // 2, local), 1), slice(None))
                out[spot] = tail[None, 8 + w : 9 + w, :] * scales[1]
            lines[pl.ds(p, 1), :] = tail[10:11, :] + tail[11:12, :]
    total = jnp.sum(lines[...], axis=0, keepdims=True) * scales[2]
    count = cols_out.shape[0]
    for r in range(count):
        cols_out[r : r + 1, :] = total[:, r * count : (r + 1) * count]


def unpack(n, rows, local, scales, place, held, cols):
    deep, size = held[0].shape[1:]
    high = (deep - 16) // 2
    return pl.pallas_call(
        functools.partial(unpack_kernel, n, scales),
        out_shape=[shape_of((4 * n * high, size), F)] * 2
        + [shape_of((cols, cols), F)]
        + [shape_of((2 * local, local, size), F)] * 2
        + [shape_of((n * rows, n * rows), F)],
        in_specs=[SM] + [VM] * 4,
        out_specs=[VM] * 6,
        scratch_shapes=[pltpu.VMEM((4 * n, size), F)],
        compiler_params=PARAMS,
        name="unpack",
    )(place, *held)


def finish_kernel(*refs):
    grads, (back, out) = refs[:-2], refs[-2:]
    n, rows, cw = back.shape[:3]
    for i in range(n):
        spot = slice(i * cw, (i + 1) * cw)
        for h in range(rows):
            out[h, spot, :] = (grads[h][spot, :].astype(F) + back[i, h].astype(F)).astype(BF)


def finish(grads, back):
    cols, width = grads[0].shape
    n, rows, cw = back.shape[:3]
    lanes = 512
    return pl.pallas_call(
        finish_kernel,
        out_shape=shape_of((rows, cols, width)),
        grid=(width // lanes,),
        in_specs=[pl.BlockSpec((cols, lanes), lambda j: (0, j))] * rows
        + [pl.BlockSpec((n, rows, cw, lanes), lambda j: (0, 0, 0, j))],
        out_specs=pl.BlockSpec((rows, cols, lanes), lambda j: (0, 0, j)),
        name="finish",
    )(*grads, back)


def shifted(value, by, n):
    return lax.ppermute(value, "seq", [(i, (i + by) % n) for i in range(n)])


def swapped(value, axis, bit, n):
    return lax.ppermute(value, axis, [(i, i ^ bit) for i in range(n)])


def traded(value):
    return lax.all_to_all(value, "seq", split_axis=0, concat_axis=0, tiled=True)


def pick(value, index):
    return lax.dynamic_index_in_dim(value, index, 0, keepdims=False)


def add(*values):
    return sum(value.astype(F) for value in values).astype(BF)


def two_lines(line):
    upper = line.astype(BF)
    return upper, (line - upper.astype(F)).astype(BF)


def reduce_parts(kept, sent, early, later, cols_sum, place_at, n):
    seq_at, x = place_at
    deep, size = kept.shape[1:]
    sent, _ = lax.optimization_barrier((sent, early))
    got = swapped(sent, "dp", 1, 4)
    halves = add(kept, got).reshape(2, n, deep, size)
    got = swapped(pick(halves, 1 - x), "dp", 2, 4)
    fours = add(pick(halves, x), got)
    got = [shifted(pick(fours, lax.rem(seq_at + i, n)), i, n) for i in range(1, n)]
    got, _ = lax.optimization_barrier((got, later))
    mine = add(pick(fours, seq_at), *got)
    tail = mine[deep - 16 :]
    count = cols_sum.size
    line = jnp.pad(cols_sum.reshape(1, count), ((0, 0), (0, size - count)))
    blank = jnp.zeros((4, size), BF)
    tail = jnp.concatenate([tail[:10], *two_lines(line), blank], axis=0)
    other = swapped(tail, "chan", 1, 2)
    both = tail.astype(F) + other.astype(F)
    lines = two_lines(both[10:11] + both[11:12])
    tail = jnp.concatenate([both[:8].astype(BF), tail[8:10], *lines, blank], axis=0)
    mine = jnp.concatenate([mine[: deep - 16], tail], axis=0)
    held = jnp.stack([mine] + [shifted(mine, i, n) for i in range(1, n)])
    return held, swapped(held, "dp", 2, 4), swapped(held, "dp", 1, 4)


def block_body(inputs, cotangent, rows_in, cols_mix, blocks_gate, blocks_up, mix_gate, mix_up):
    n = lax.axis_size("seq")
    rows, cols, width = inputs.shape[1:]
    local, size = blocks_gate.shape[:2]
    cw = cols // n
    seq_at, chan_at, dp_at = lax.axis_index("seq"), lax.axis_index("chan"), lax.axis_index("dp")
    core, x = lax.rem(dp_at, 2), dp_at // 2
    place = jnp.stack([seq_at, chan_at, core, x]).astype(jnp.int32)
    values, cot = inputs[0], cotangent[0]
    ahead, behind = mix_tables(cols_mix, rows, cw)

    def relative(table):
        turned = jnp.roll(table, (local, local), (0, 1))
        table = jnp.where(chan_at == 0, table, turned).astype(F)
        return jnp.broadcast_to(table[:, :, None, :], table.shape[:2] + (8, size))

    x_cols = traded(values.reshape(rows, n, cw, width).transpose(1, 0, 2, 3))
    cot_oth = swapped(cot, "chan", 1, 2)
    lent = jnp.where(core == 0, blocks_gate, blocks_up)
    lent, _ = lax.optimization_barrier((lent, cot_oth))
    lent = swapped(lent, "chan", 1, 2)
    lent_too = swapped(lent, "dp", 1, 4)
    gate_oth = jnp.where(core == 0, lent, lent_too)
    up_oth = jnp.where(core == 0, lent_too, lent)
    weights = (blocks_gate, gate_oth, blocks_up, up_oth)
    mixes = (relative(mix_gate), relative(mix_up))

    x_cols, ahead, behind, mixes, cot_oth = lax.optimization_barrier(
        (x_cols, ahead, behind, mixes, cot_oth)
    )
    parts = column_mix(ahead, x_cols.reshape(n * rows * cw, width))
    mixed = [traded(part.reshape(n, cw, width)).reshape(cols, width) for part in parts]
    hidden = [hidden_row(rows_in, values, h, mixed[h]) for h in range(rows)]
    leaving = list(hidden)
    leaving[0], _ = lax.optimization_barrier((leaving[0], lent))
    others = [swapped(hid, "chan", 1, 2) for hid in leaving]
    others[0], hidden[-1] = lax.optimization_barrier((others[0], hidden[-1]))
    grads, back_g, back_u, mix_sum, pieces = [], [], [], [], []
    for h in range(rows):
        got = channel_row(h, hidden[h], others[h], cot, cot_oth, weights, mixes, rows_in)
        for held, value in zip((grads, back_g, back_u, pieces, mix_sum), got):
            held.append(value)
        if h == 0:
            pieces[0], others[-1] = lax.optimization_barrier((pieces[0], others[-1]))
        pieces[h] = traded(pieces[h].reshape(n, cw, width))
    kept, sent = sums(place, 4 * n, hidden, back_g, back_u, grads, mixed, mix_sum)
    flat = [piece.reshape(cols, width) for piece in pieces]
    turned = column_back(behind, flat)
    back = traded(turned.reshape(n, rows, cw, width))
    cols_sum = column_sum(x_cols, pieces)
    cols_sum = cols_sum.reshape(n * rows, n * rows, cw).sum(-1)
    batch_all = lax.axis_size("dp")
    width_all = width * lax.axis_size("chan")
    rows_scale = 1.0 / math.sqrt(batch_all * rows * n * width_all)
    cols_scale = 1.0 / math.sqrt(batch_all * cols * width_all)
    block_scale = 1.0 / math.sqrt(batch_all * rows * n * cols)
    held, by_x, by_core = reduce_parts(kept, sent, pieces[0], turned, cols_sum, (seq_at, x), n)
    input_grad = finish(grads, back)
    by_x, input_grad = lax.optimization_barrier((by_x, input_grad))
    gate_sum, up_sum, rows_sum, mix_g, mix_u, cols_sum = unpack(
        n,
        rows,
        local,
        (rows_scale, block_scale, cols_scale),
        place,
        (held, by_x, by_core, swapped(by_x, "dp", 1, 4)),
        cols,
    )
    return (
        input_grad[None],
        rows_sum,
        cols_sum,
        gate_sum.reshape(local, size, size),
        up_sum.reshape(local, size, size),
        mix_g,
        mix_u,
    )


def column_keep(segment, cols_mix):
    mixed = jnp.einsum(
        "er,brcd->becd", cols_mix, segment, preferred_element_type=jnp.float32
    ).astype(jnp.bfloat16)
    return (segment, mixed)

def body(inputs, cotangent, rows_in, cols_mix, blocks_gate, blocks_up, mix_gate, mix_up):
    batch_dev, rows_dev, cols_all, width_dev = inputs.shape
    block_size = blocks_gate.shape[1]
    local_blocks = blocks_gate.shape[0]
    chan_index = lax.axis_index("chan")
    split_shape = (batch_dev, rows_dev, cols_all, local_blocks, block_size)
    first = jnp.einsum("ec,brcd->bred", rows_in, inputs, preferred_element_type=jnp.float32).astype(
        jnp.bfloat16
    )
    first_cols, second_cols = column_keep(
        lax.all_to_all(first, "seq", split_axis=2, concat_axis=1, tiled=True), cols_mix
    )
    second_rows = lax.all_to_all(second_cols, "seq", split_axis=1, concat_axis=2, tiled=True)
    hidden = (inputs.astype(jnp.float32) + second_rows.astype(jnp.float32)).astype(jnp.bfloat16)
    hidden_blocks = hidden.reshape(split_shape)
    gate_rows_own = lax.dynamic_slice_in_dim(
        mix_gate, chan_index * local_blocks, local_blocks, 0
    ).astype(jnp.float32)
    up_rows_own = lax.dynamic_slice_in_dim(
        mix_up, chan_index * local_blocks, local_blocks, 0
    ).astype(jnp.float32)
    gate_mid = jnp.einsum(
        "brckj,kjl->brckl", hidden_blocks, blocks_gate, preferred_element_type=jnp.float32
    ).astype(jnp.bfloat16)
    up_mid = jnp.einsum(
        "brckj,kjl->brckl", hidden_blocks, blocks_up, preferred_element_type=jnp.float32
    ).astype(jnp.bfloat16)
    gate_add = jnp.einsum(
        "mkj,brckj->brcmj",
        gate_rows_own,
        lax.all_gather(gate_mid, "chan", axis=3, tiled=True).astype(jnp.float32),
    )
    up_add = jnp.einsum(
        "mkj,brckj->brcmj",
        up_rows_own,
        lax.all_gather(up_mid, "chan", axis=3, tiled=True).astype(jnp.float32),
    )
    upstream = cotangent.astype(jnp.float32).reshape(split_shape)
    sigma = jax.nn.sigmoid(gate_add)
    up_grad = (upstream * gate_add * sigma).astype(jnp.bfloat16)
    gate_grad = (upstream * up_add * sigma * (1.0 + gate_add * (1.0 - sigma))).astype(jnp.bfloat16)
    gate_all, up_all = (
        lax.all_gather(gate_grad, "chan", axis=3, tiled=True),
        lax.all_gather(up_grad, "chan", axis=3, tiled=True),
    )
    gate_cols_own = lax.dynamic_slice_in_dim(
        mix_gate, chan_index * local_blocks, local_blocks, 1
    ).astype(jnp.float32)
    up_cols_own = lax.dynamic_slice_in_dim(
        mix_up, chan_index * local_blocks, local_blocks, 1
    ).astype(jnp.float32)
    mix_gate_sum = jnp.einsum(
        "brcmj,brckj->mkj", gate_all, gate_mid, preferred_element_type=jnp.float32
    )
    mix_up_sum = jnp.einsum("brcmj,brckj->mkj", up_all, up_mid, preferred_element_type=jnp.float32)
    gate_back = jnp.einsum("mkj,brcmj->brckj", gate_cols_own, gate_all.astype(jnp.float32)).astype(
        jnp.bfloat16
    )
    up_back = jnp.einsum("mkj,brcmj->brckj", up_cols_own, up_all.astype(jnp.float32)).astype(
        jnp.bfloat16
    )
    blocks_gate_sum = jnp.einsum(
        "brckj,brckl->kjl", hidden_blocks, gate_back, preferred_element_type=jnp.float32
    )
    blocks_up_sum = jnp.einsum(
        "brckj,brckl->kjl", hidden_blocks, up_back, preferred_element_type=jnp.float32
    )
    hidden_grad = (
        upstream
        + jnp.einsum("brckl,kjl->brckj", gate_back, blocks_gate, preferred_element_type=jnp.float32)
        + jnp.einsum("brckl,kjl->brckj", up_back, blocks_up, preferred_element_type=jnp.float32)
    )
    hidden_grad = hidden_grad.reshape(inputs.shape).astype(jnp.bfloat16)
    segment = lax.all_to_all(hidden_grad, "seq", split_axis=2, concat_axis=1, tiled=True)
    mixed = jnp.einsum(
        "er,becd->brcd", cols_mix, segment, preferred_element_type=jnp.float32
    ).astype(jnp.bfloat16)
    cols_sum = jnp.einsum("becd,brcd->er", segment, first_cols, preferred_element_type=jnp.float32)
    first_grad = lax.all_to_all(mixed, "seq", split_axis=1, concat_axis=2, tiled=True)
    rows_sum = jnp.einsum("bred,brcd->ec", first_grad, inputs, preferred_element_type=jnp.float32)
    input_grad = (
        hidden_grad.astype(jnp.float32)
        + jnp.einsum("ec,bred->brcd", rows_in, first_grad, preferred_element_type=jnp.float32)
    ).astype(jnp.bfloat16)
    rows_total, cols_total = lax.psum((rows_sum, cols_sum), ("dp", "seq", "chan"))
    gate_blocks_total, up_blocks_total, gate_mix_total, up_mix_total = lax.psum(
        (blocks_gate_sum, blocks_up_sum, mix_gate_sum, mix_up_sum), ("dp", "seq")
    )
    count_dp = lax.axis_size("dp")
    count_seq = lax.axis_size("seq")
    count_chan = lax.axis_size("chan")
    batch_all = batch_dev * count_dp
    rows_all = rows_dev * count_seq
    width_all = width_dev * count_chan
    rows_scale = 1.0 / math.sqrt(batch_all * rows_all * width_all)
    cols_scale = 1.0 / math.sqrt(batch_all * cols_all * width_all)
    block_scale = 1.0 / math.sqrt(batch_all * rows_all * cols_all)
    return (
        input_grad,
        rows_total * rows_scale,
        cols_total * cols_scale,
        gate_blocks_total * block_scale,
        up_blocks_total * block_scale,
        gate_mix_total * block_scale,
        up_mix_total * block_scale,
    )


def solution(mesh):
    in_specs = (
        P("dp", "seq", None, "chan"),
        P("dp", "seq", None, "chan"),
        P(),
        P(),
        P("chan", None, None),
        P("chan", None, None),
        P(),
        P(),
    )
    out_specs = (
        P("dp", "seq", None, "chan"),
        P(),
        P(),
        P("chan", None, None),
        P("chan", None, None),
        P(None, "chan", None),
        P(None, "chan", None),
    )
    sizes = dict(mesh.shape)
    fits = sizes["dp"] == 4 and sizes["seq"] == 4 and sizes["chan"] == 2
    return jax.shard_map(block_body if fits else body, mesh=mesh, in_specs=in_specs, out_specs=out_specs, check_vma=False)
```

```python
import functools
import math

import jax
import jax.numpy as jnp
from jax import lax
from jax.experimental import pallas as pl
from jax.experimental.pallas import tpu as pltpu
from jax.sharding import PartitionSpec as P

BF = jnp.bfloat16
F = jnp.float32
VM = pl.BlockSpec(memory_space=pltpu.VMEM)
SM = pl.BlockSpec(memory_space=pltpu.SMEM)
PARAMS = pltpu.CompilerParams(vmem_limit_bytes=20 * 1024 * 1024)


def whole(*dims):
    return pl.BlockSpec(dims, lambda j: (0,) * len(dims))


def wholes(*values):
    return [whole(*value.shape) for value in values]


def once(kernel):
    def run(*refs):
        @pl.when(pl.program_id(0) == 0)
        def _():
            kernel(*refs)

    return run


def held_in_hbm(*values):
    return [pltpu.with_memory_space_constraint(value, pltpu.HBM) for value in values]


def shape_of(dims, kind=BF):
    return pltpu.HBM(dims, kind)


def turned_blocks(table, at, n, rows):
    return jnp.concatenate(
        [
            lax.dynamic_slice_in_dim(table, lax.rem(at + n - j, n) * rows, rows, 1)
            for j in range(n)
        ],
        axis=1,
    )


def mix_tables(mix, at, n, rows, cw):
    same = lax.broadcasted_iota(jnp.int32, (1, cw, 1, cw), 1) == lax.broadcasted_iota(
        jnp.int32, (1, cw, 1, cw), 3
    )

    def spread(table):
        grown = jnp.where(same, table[:, None, :, None], jnp.zeros((), BF))
        return grown.reshape(table.shape[0] * cw, table.shape[1] * cw)

    ahead = turned_blocks(mix, at, n, rows)
    ahead = jnp.stack([spread(ahead[h::rows]) for h in range(rows)])
    by_row = mix.reshape(n, rows, -1).transpose(1, 0, 2).reshape(mix.shape)
    back = jnp.stack([spread(by_row[:, h::rows].T) for h in range(rows)])
    return ahead, back


def column_mix_kernel(rows, table, *refs):
    sources, outs = refs[:-rows], refs[-rows:]
    for h in range(rows):
        total = None
        for j, source in enumerate(sources):
            deep = source.shape[0]
            term = jnp.dot(
                table[h, :, j * deep : (j + 1) * deep], source[...], preferred_element_type=F
            )
            total = term if total is None else total + term
        outs[h][...] = total.astype(BF)


def column_mix(table, sources, name):
    rows, deep, size = table.shape
    width = sources[0].shape[-1]
    lanes = 512
    return pl.pallas_call(
        functools.partial(column_mix_kernel, rows),
        out_shape=[shape_of((deep, width))] * rows,
        grid=(width // lanes,),
        in_specs=[pl.BlockSpec((rows, deep, size), lambda j: (0, 0, 0))]
        + [pl.BlockSpec((source.shape[0], lanes), lambda j: (0, j)) for source in sources],
        out_specs=[pl.BlockSpec((deep, lanes), lambda j: (0, j))] * rows,
        name=name,
    )(*held_in_hbm(table, *sources))


def column_sum_kernel(cw, rows, *refs):
    pieces, sources, (out, left, right) = refs[:rows], refs[rows:-3], refs[-3:]
    for side, parts in ((left, pieces), (right, sources)):
        deep = parts[0].shape[0]
        for j, part in enumerate(parts):
            side[j * deep : (j + 1) * deep, :] = part[...]
    product = lax.dot_general(
        left[...], right[...], (((1,), (1,)), ((), ())), preferred_element_type=F
    )
    size = product.shape[0]
    row_at = lax.broadcasted_iota(jnp.int32, (size, size), 0)
    col_at = lax.broadcasted_iota(jnp.int32, (size, size), 1)
    kept = jnp.where(lax.rem(row_at, cw) == lax.rem(col_at, cw), product, 0.0)
    out[...] = jnp.sum(kept.reshape(size // cw, cw, size), axis=1)


def column_sum(cw, sources, pieces):
    width = pieces[0].shape[1]
    size = sum(piece.shape[0] for piece in pieces)
    return pl.pallas_call(
        once(functools.partial(column_sum_kernel, cw, len(pieces))),
        out_shape=shape_of((size // cw, size), F),
        grid=(2,),
        in_specs=wholes(*pieces, *sources),
        out_specs=whole(size // cw, size),
        scratch_shapes=[pltpu.VMEM((size, width), BF)] * 2,
        compiler_params=PARAMS,
        name="column_sum",
    )(*held_in_hbm(*pieces, *sources))


def hidden_kernel(rows_in, x, mixed, hidden):
    second = jnp.dot(rows_in[...], mixed[...], preferred_element_type=F)
    hidden[...] = (x[...].astype(F) + second).astype(BF)


def hidden_row(rows_in, inputs, h, mixed):
    cols, width = mixed.shape
    lanes = 512
    column = pl.BlockSpec((cols, lanes), lambda j: (0, j))
    return pl.pallas_call(
        hidden_kernel,
        out_shape=shape_of((cols, width)),
        grid=(width // lanes,),
        in_specs=[
            pl.BlockSpec((cols, cols), lambda j: (0, 0)),
            pl.BlockSpec((None, cols, lanes), lambda j: (h, 0, j)),
            column,
        ],
        out_specs=column,
        name="hidden_row",
    )(*held_in_hbm(rows_in, inputs, mixed))


def channel_kernel(first, *refs):
    (place, h_own, h_oth, c_own, c_oth, wg_own, wu_own, lent, lent_too, mix_g, mix_u) = refs[:11]
    rows_in, mixed, *before = refs[11 : 13 if first else 14]
    hid_grad, back_g, back_u, turned, mix_sum, row_sum, mid_g, mid_u = refs[-8:]
    local, size = wg_own.shape[:2]
    blocks = 2 * local
    cols = h_own.shape[0]

    def middle(base, h, wg, wu):
        for k in range(local):
            part = h[:, k * size : (k + 1) * size]
            mid_g[base + k] = jnp.dot(part, wg[k], preferred_element_type=F)
            mid_u[base + k] = jnp.dot(part, wu[k], preferred_element_type=F)

    middle(0, h_own, wg_own, wu_own)

    @pl.when(place[2] == 0)
    def _():
        middle(local, h_oth, lent, lent_too)

    @pl.when(place[2] != 0)
    def _():
        middle(local, h_oth, lent_too, lent)

    mix_sum[...] = jnp.zeros_like(mix_sum)
    deep, lanes = 16, 128

    def chunk(t, carry):
        rows = pl.ds(pl.multiple_of(t * deep, deep), deep)
        for q in range(size // lanes):
            at = slice(q * lanes, (q + 1) * lanes)
            shape = (deep // 8, 8, lanes)
            g = [mid_g[k, rows, at].reshape(shape) for k in range(blocks)]
            u = [mid_u[k, rows, at].reshape(shape) for k in range(blocks)]
            sum_g, sum_u = [None] * local, [None] * local
            for m in range(blocks):
                c = c_own if m < local else c_oth
                start = (m % local) * size + q * lanes
                up = c[rows, start : start + lanes].astype(F).reshape(shape)
                gate_out = mix_g[m, 0, :, at] * g[0]
                up_out = mix_u[m, 0, :, at] * u[0]
                for k in range(1, blocks):
                    gate_out = gate_out + mix_g[m, k, :, at] * g[k]
                    up_out = up_out + mix_u[m, k, :, at] * u[k]
                sigma = 0.5 * jnp.tanh(0.5 * gate_out) + 0.5
                scaled = up * sigma
                up_grad = scaled * gate_out
                gate_grad = scaled * up_out * (1.0 + gate_out * (1.0 - sigma))
                for k in range(local):
                    mix_sum[0, m, k, :, at] += jnp.sum(gate_grad * g[k], axis=0)
                    mix_sum[1, m, k, :, at] += jnp.sum(up_grad * u[k], axis=0)
                    term_g = mix_g[m, k, :, at] * gate_grad
                    term_u = mix_u[m, k, :, at] * up_grad
                    sum_g[k] = term_g if m == 0 else sum_g[k] + term_g
                    sum_u[k] = term_u if m == 0 else sum_u[k] + term_u
            for k in range(local):
                spot = slice(k * size + q * lanes, k * size + (q + 1) * lanes)
                back_g[rows, spot] = sum_g[k].reshape(deep, lanes).astype(BF)
                back_u[rows, spot] = sum_u[k].reshape(deep, lanes).astype(BF)
        return carry

    lax.fori_loop(0, cols // deep, chunk, 0)
    last = (((1,), (1,)), ((), ()))
    for k in range(local):
        spot = slice(k * size, (k + 1) * size)
        grad = lax.dot_general(back_g[:, spot], wg_own[k], last, preferred_element_type=F)
        grad = grad + lax.dot_general(back_u[:, spot], wu_own[k], last, preferred_element_type=F)
        hid_grad[:, spot] = (c_own[:, spot].astype(F) + grad).astype(BF)
    turned[...] = lax.dot_general(
        rows_in[...], hid_grad[...], (((0,), (0,)), ((), ())), preferred_element_type=F
    ).astype(BF)
    total = lax.dot_general(hid_grad[...], mixed[...], last, preferred_element_type=F)
    for held in before:
        total = held[...] + total
    row_sum[...] = total


def channel_row(place, h, h_own, h_oth, cot, cot_oth, weights, mixes, rows_in, mixed, before):
    cols, width = h_own.shape
    local, size = weights[0].shape[:2]
    blocks = 2 * local
    row = pl.BlockSpec((None, cols, width), lambda j: (h, 0, 0))
    return pl.pallas_call(
        once(functools.partial(channel_kernel, not before)),
        out_shape=[shape_of((cols, width))] * 4
        + [shape_of((2, blocks, local, 8, size), F), shape_of((cols, cols), F)],
        grid=(2,),
        in_specs=[SM]
        + wholes(h_own, h_oth)
        + [row, row]
        + [VM] * 7
        + wholes(mixed, *before),
        out_specs=[whole(cols, width)] * 4
        + [whole(2, blocks, local, 8, size), whole(cols, cols)],
        scratch_shapes=[pltpu.VMEM((blocks, cols, size), F)] * 2,
        compiler_params=PARAMS,
        name="channel_row",
    )(
        place,
        *held_in_hbm(h_own, h_oth, cot, cot_oth),
        *weights,
        *mixes,
        rows_in,
        *held_in_hbm(mixed, *before),
    )


def sums_kernel(rows, parts, place, row_sum, *refs):
    hid, back_g, back_u, mix_sum = (refs[i * rows : (i + 1) * rows] for i in range(4))
    outs = refs[4 * rows :]
    size = outs[0].shape[-1]
    local = hid[0].shape[1] // size
    blocks = 2 * local
    first = (((0,), (0,)), ((), ()))
    high = local * size // parts
    per = size // high
    chan, core = place[1], place[2]
    for part, out in ((1, outs[1]), (0, outs[0])):
        k = core if part == 0 else 1 - core
        spot = pl.ds(pl.multiple_of(k * size, size), size)
        for w, back in enumerate((back_g, back_u)):
            total = None
            for h in range(rows):
                term = lax.dot_general(
                    hid[h][:, spot], back[h][:, spot], first, preferred_element_type=F
                )
                total = term if total is None else total + term
            for q in range(per):
                out[q, w * high : (w + 1) * high, :] = total[q * high : (q + 1) * high].astype(BF)
        for q in range(per):
            p = k * per + q
            m_at = lax.rem(p // (2 * local) + blocks - chan * local, blocks)
            k_at = lax.rem(p // 2, local)
            lines = [
                jnp.sum(sum(ref[w, m_at, k_at] for ref in mix_sum), axis=0, keepdims=True)
                for w in range(2)
            ]
            at = pl.multiple_of(p * 16, 16)
            eight = jnp.concatenate(
                [row_sum[pl.ds(at, 8), :], row_sum[pl.ds(at + 8, 8), :]], axis=1
            )
            tail = jnp.concatenate([eight, *lines, jnp.zeros((6, size), F)], axis=0)
            out[q, 2 * high :, :] = tail.astype(BF)


def sums(place, parts, row_sum, hid, back_g, back_u, mix_sum):
    rows = len(hid)
    size = mix_sum[0].shape[-1]
    high = hid[0].shape[1] // parts
    dims = (parts // 2, 2 * high + 16, size)
    return pl.pallas_call(
        once(functools.partial(sums_kernel, rows, parts)),
        out_shape=[shape_of(dims)] * 2,
        grid=(2,),
        in_specs=[SM] + wholes(row_sum, *hid, *back_g, *back_u, *mix_sum),
        out_specs=[whole(*dims)] * 2,
        compiler_params=PARAMS,
        name="sums",
    )(place, *held_in_hbm(row_sum, *hid, *back_g, *back_u, *mix_sum))


def core_add_kernel(n, place, kept, got, *outs):
    at, x = place[0], place[3]
    for i in range(n):
        for part in range(2):
            q = (x if part else 1 - x) * n + lax.rem(at + i, n)
            out = outs[n].at[i] if part else outs[i]
            out[...] = (kept[q].astype(F) + got[q].astype(F)).astype(BF)


def core_add(n, place, kept, got):
    deep, size = kept.shape[1:]
    return pl.pallas_call(
        once(functools.partial(core_add_kernel, n)),
        out_shape=[shape_of((deep, size))] * n + [shape_of((n, deep, size))],
        grid=(2,),
        in_specs=[SM] + wholes(kept, got),
        out_specs=[whole(deep, size)] * n + [whole(n, deep, size)],
        compiler_params=PARAMS,
        name="core_add",
    )(place, *held_in_hbm(kept, got))


def unpack_kernel(n, scales, place, *refs):
    held = refs[:4]
    gate, up, rows, mix_g, mix_u, cols_out, lines = refs[4:]
    local = mix_g.shape[1]
    at, core, x = place[0], place[2], place[3]
    high = gate.shape[0] // (4 * n)
    half = rows.shape[1]
    for i in range(4):
        base = lax.rem(core + i // 2, 2) * 2 * n + lax.rem(x + i % 2, 2) * n
        for j in range(n):
            p = base + lax.rem(at + n - j, n)
            spot = pl.ds(pl.multiple_of(p * high, high), high)
            gate[spot, :] = held[i][j, :high, :].astype(F) * scales[1]
            up[spot, :] = held[i][j, high : 2 * high, :].astype(F) * scales[1]
            tail = held[i][j, 2 * high :, :].astype(F)
            where = pl.multiple_of(p * 16, 16)
            rows[pl.ds(where, 8), :] = tail[:8, :half] * scales[0]
            rows[pl.ds(where + 8, 8), :] = tail[:8, half:] * scales[0]
            for w, out in enumerate((mix_g, mix_u)):
                spot = (pl.ds(p // (2 * local), 1), pl.ds(lax.rem(p // 2, local), 1), slice(None))
                out[spot] = tail[None, 8 + w : 9 + w, :] * scales[1]
            lines[pl.ds(p, 1), :] = tail[10:11, :] + tail[11:12, :]
    total = jnp.sum(lines[...], axis=0, keepdims=True) * scales[2]
    count = cols_out.shape[0]
    for r in range(count):
        cols_out[r : r + 1, :] = total[:, r * count : (r + 1) * count]


def unpack(n, rows, local, scales, place, held, cols):
    deep, size = held[0].shape[1:]
    high = (deep - 16) // 2
    return pl.pallas_call(
        functools.partial(unpack_kernel, n, scales),
        out_shape=[shape_of((4 * n * high, size), F)] * 2
        + [shape_of((cols, cols), F)]
        + [shape_of((2 * local, local, size), F)] * 2
        + [shape_of((n * rows, n * rows), F)],
        grid=(1,),
        in_specs=[SM] + wholes(*held),
        out_specs=[whole(4 * n * high, size)] * 2
        + [whole(cols, cols)]
        + [whole(2 * local, local, size)] * 2
        + [whole(n * rows, n * rows)],
        scratch_shapes=[pltpu.VMEM((4 * n, size), F)],
        compiler_params=PARAMS,
        name="unpack",
    )(place, *held_in_hbm(*held))


def finish_kernel(rows, *refs):
    grads, backs, out = refs[:rows], refs[rows:-1], refs[-1]
    for h in range(rows):
        out[h] = (grads[h][...].astype(F) + backs[h][...].astype(F)).astype(BF)


def finish(grads, backs):
    rows = len(grads)
    cols, width = grads[0].shape
    lanes = 512
    column = pl.BlockSpec((cols, lanes), lambda j: (0, j))
    return pl.pallas_call(
        functools.partial(finish_kernel, rows),
        out_shape=shape_of((rows, cols, width)),
        grid=(width // lanes,),
        in_specs=[column] * (2 * rows),
        out_specs=pl.BlockSpec((rows, cols, lanes), lambda j: (0, 0, j)),
        name="finish",
    )(*held_in_hbm(*grads, *backs))


def shifted(value, by, n):
    return lax.ppermute(value, "seq", [(i, (i + by) % n) for i in range(n)])


def swapped(value, axis, bit, n):
    return lax.ppermute(value, axis, [(i, i ^ bit) for i in range(n)])


def traded(value):
    return lax.all_to_all(value, "seq", split_axis=0, concat_axis=0, tiled=True)


def pick(value, index):
    return lax.dynamic_index_in_dim(value, index, 0, keepdims=False)


def add(*values):
    return sum(value.astype(F) for value in values).astype(BF)


def two_lines(line):
    upper = line.astype(BF)
    return upper, (line - upper.astype(F)).astype(BF)


def two_lines(line):
    upper = line.astype(BF)
    return upper, (line - upper.astype(F)).astype(BF)


def scatter_seq(by_x, fours, cols_sum, n):
    deep, size = fours.shape[1:]
    arrived = []
    for i in [*range(1, n), 0]:
        shard = add(fours[i], by_x[i])
        arrived.append(shifted(shard, i, n) if i else shard)
    count = cols_sum.size
    line = jnp.pad(cols_sum.reshape(1, count), ((0, 0), (0, size - count)))
    lines = jnp.pad(jnp.concatenate(two_lines(line), axis=0), ((deep - 6, 4), (0, 0)))
    mine = add(*arrived, lines)
    tail = mine[deep - 16 :]
    other = swapped(tail, "chan", 1, 2)
    both = tail.astype(F) + other.astype(F)
    lines = two_lines(both[10:11] + both[11:12])
    tail = jnp.concatenate([both[:8].astype(BF), tail[8:10], *lines, tail[12:]], axis=0)
    return jnp.concatenate([mine[: deep - 16], tail], axis=0)


def block_body(inputs, cotangent, rows_in, cols_mix, blocks_gate, blocks_up, mix_gate, mix_up):
    n = lax.axis_size("seq")
    rows, cols, width = inputs.shape[1:]
    local, size = blocks_gate.shape[:2]
    cw = cols // n
    seq_at, chan_at, dp_at = lax.axis_index("seq"), lax.axis_index("chan"), lax.axis_index("dp")
    core, x = lax.rem(dp_at, 2), dp_at // 2
    place = jnp.stack([seq_at, chan_at, core, x]).astype(jnp.int32)
    values, cot = inputs[0], cotangent[0]
    ahead, behind = mix_tables(cols_mix, seq_at, n, rows, cw)

    def relative(table):
        turned = jnp.roll(table, (local, local), (0, 1))
        table = jnp.where(chan_at == 0, table, turned).astype(F)
        return jnp.broadcast_to(table[:, :, None, :], table.shape[:2] + (8, size))

    ways = [
        lax.dynamic_slice_in_dim(values, lax.rem(seq_at + i, n) * cw, cw, 1) for i in range(n)
    ]
    x_cols = [ways[0]] + [shifted(ways[i], i, n) for i in range(1, n)]
    x_cols = [part.reshape(rows * cw, width) for part in x_cols]
    cot_oth = swapped(cot, "chan", 1, 2)
    lent = jnp.where(core == 0, blocks_gate, blocks_up)
    lent, _ = lax.optimization_barrier((lent, cot_oth))
    lent = swapped(lent, "chan", 1, 2)
    mixes = (relative(mix_gate), relative(mix_up))

    x_cols, ahead, behind, mixes = lax.optimization_barrier((x_cols, ahead, behind, mixes))
    parts = column_mix(ahead, x_cols, "column_mix")
    parts, cot_oth = lax.optimization_barrier((parts, cot_oth))
    mixed = [traded(part.reshape(n, cw, width)).reshape(cols, width) for part in parts]
    hidden = [hidden_row(rows_in, values, h, mixed[h]) for h in range(rows)]
    leaving = list(hidden)
    lender, _ = lax.optimization_barrier((lent, hidden[0]))
    lent_too = swapped(lender, "dp", 1, 4)
    weights = (blocks_gate, blocks_up, lent, lent_too)
    leaving[0], _ = lax.optimization_barrier((leaving[0], lent))
    others = [swapped(hid, "chan", 1, 2) for hid in leaving]
    others[0], hidden[-1] = lax.optimization_barrier((others[0], hidden[-1]))
    grads, back_g, back_u, pieces, mix_sum, rows_sum = [], [], [], [], [], []
    for h in range(rows):
        got = channel_row(
            place,
            h,
            hidden[h],
            others[h],
            cot,
            cot_oth,
            weights,
            mixes,
            rows_in,
            mixed[h],
            rows_sum,
        )
        for held, value in zip((grads, back_g, back_u, pieces, mix_sum), got):
            held.append(value)
        rows_sum = got[5:]
    kept, sent = sums(place, 4 * n, rows_sum[0], hidden, back_g, back_u, mix_sum)
    pieces[0], _ = lax.optimization_barrier((pieces[0], others[-1]))
    pieces[0] = traded(pieces[0].reshape(n, cw, width)).reshape(cols, width)
    sent, _ = lax.optimization_barrier((sent, pieces[0]))
    pieces[1], _ = lax.optimization_barrier((pieces[1], kept))
    pieces[1] = traded(pieces[1].reshape(n, cw, width)).reshape(cols, width)
    *leaving, fours = core_add(n, place, kept, swapped(sent, "dp", 1, 4))
    by_x = [swapped(shard, "dp", 2, 4) for shard in leaving]
    pieces[1], _ = lax.optimization_barrier((pieces[1], by_x[1]))
    turned = column_mix(behind, pieces, "column_back")
    backs = [traded(turned[0].reshape(n, cw, width))]
    late, _ = lax.optimization_barrier((pieces[1], turned[0]))
    cols_sum = column_sum(cw, x_cols, [pieces[0], late])
    cols_sum = cols_sum.reshape(rows, n, n * rows, cw).sum(-1).transpose(1, 0, 2)
    cols_sum = turned_blocks(cols_sum.reshape(n * rows, n * rows), seq_at, n, rows)
    mine = scatter_seq(by_x, fours, cols_sum, n)
    held = [mine] + [shifted(mine, i, n) for i in range(1, n)]
    for part in turned[1:]:
        part, _ = lax.optimization_barrier((part, held[1:]))
        backs.append(traded(part.reshape(n, cw, width)))
    backs = [part.reshape(cols, width) for part in backs]
    batch_all = lax.axis_size("dp")
    width_all = width * lax.axis_size("chan")
    rows_scale = 1.0 / math.sqrt(batch_all * rows * n * width_all)
    cols_scale = 1.0 / math.sqrt(batch_all * cols * width_all)
    block_scale = 1.0 / math.sqrt(batch_all * rows * n * cols)
    by_x = jnp.stack([swapped(shard, "dp", 2, 4) for shard in held])
    held = jnp.stack(held)
    by_core = swapped(held, "dp", 1, 4)
    input_grad = finish(grads, backs)
    gate_sum, up_sum, rows_sum, mix_g, mix_u, cols_sum = unpack(
        n,
        rows,
        local,
        (rows_scale, block_scale, cols_scale),
        place,
        (held, by_x, by_core, swapped(by_x, "dp", 1, 4)),
        cols,
    )
    return (
        input_grad[None],
        rows_sum,
        cols_sum,
        gate_sum.reshape(local, size, size),
        up_sum.reshape(local, size, size),
        mix_g,
        mix_u,
    )


def column_keep(segment, cols_mix):
    mixed = jnp.einsum(
        "er,brcd->becd", cols_mix, segment, preferred_element_type=jnp.float32
    ).astype(jnp.bfloat16)
    return (segment, mixed)

def body(inputs, cotangent, rows_in, cols_mix, blocks_gate, blocks_up, mix_gate, mix_up):
    batch_dev, rows_dev, cols_all, width_dev = inputs.shape
    block_size = blocks_gate.shape[1]
    local_blocks = blocks_gate.shape[0]
    chan_index = lax.axis_index("chan")
    split_shape = (batch_dev, rows_dev, cols_all, local_blocks, block_size)
    first = jnp.einsum("ec,brcd->bred", rows_in, inputs, preferred_element_type=jnp.float32).astype(
        jnp.bfloat16
    )
    first_cols, second_cols = column_keep(
        lax.all_to_all(first, "seq", split_axis=2, concat_axis=1, tiled=True), cols_mix
    )
    second_rows = lax.all_to_all(second_cols, "seq", split_axis=1, concat_axis=2, tiled=True)
    hidden = (inputs.astype(jnp.float32) + second_rows.astype(jnp.float32)).astype(jnp.bfloat16)
    hidden_blocks = hidden.reshape(split_shape)
    gate_rows_own = lax.dynamic_slice_in_dim(
        mix_gate, chan_index * local_blocks, local_blocks, 0
    ).astype(jnp.float32)
    up_rows_own = lax.dynamic_slice_in_dim(
        mix_up, chan_index * local_blocks, local_blocks, 0
    ).astype(jnp.float32)
    gate_mid = jnp.einsum(
        "brckj,kjl->brckl", hidden_blocks, blocks_gate, preferred_element_type=jnp.float32
    ).astype(jnp.bfloat16)
    up_mid = jnp.einsum(
        "brckj,kjl->brckl", hidden_blocks, blocks_up, preferred_element_type=jnp.float32
    ).astype(jnp.bfloat16)
    gate_add = jnp.einsum(
        "mkj,brckj->brcmj",
        gate_rows_own,
        lax.all_gather(gate_mid, "chan", axis=3, tiled=True).astype(jnp.float32),
    )
    up_add = jnp.einsum(
        "mkj,brckj->brcmj",
        up_rows_own,
        lax.all_gather(up_mid, "chan", axis=3, tiled=True).astype(jnp.float32),
    )
    upstream = cotangent.astype(jnp.float32).reshape(split_shape)
    sigma = jax.nn.sigmoid(gate_add)
    up_grad = (upstream * gate_add * sigma).astype(jnp.bfloat16)
    gate_grad = (upstream * up_add * sigma * (1.0 + gate_add * (1.0 - sigma))).astype(jnp.bfloat16)
    gate_all, up_all = (
        lax.all_gather(gate_grad, "chan", axis=3, tiled=True),
        lax.all_gather(up_grad, "chan", axis=3, tiled=True),
    )
    gate_cols_own = lax.dynamic_slice_in_dim(
        mix_gate, chan_index * local_blocks, local_blocks, 1
    ).astype(jnp.float32)
    up_cols_own = lax.dynamic_slice_in_dim(
        mix_up, chan_index * local_blocks, local_blocks, 1
    ).astype(jnp.float32)
    mix_gate_sum = jnp.einsum(
        "brcmj,brckj->mkj", gate_all, gate_mid, preferred_element_type=jnp.float32
    )
    mix_up_sum = jnp.einsum("brcmj,brckj->mkj", up_all, up_mid, preferred_element_type=jnp.float32)
    gate_back = jnp.einsum("mkj,brcmj->brckj", gate_cols_own, gate_all.astype(jnp.float32)).astype(
        jnp.bfloat16
    )
    up_back = jnp.einsum("mkj,brcmj->brckj", up_cols_own, up_all.astype(jnp.float32)).astype(
        jnp.bfloat16
    )
    blocks_gate_sum = jnp.einsum(
        "brckj,brckl->kjl", hidden_blocks, gate_back, preferred_element_type=jnp.float32
    )
    blocks_up_sum = jnp.einsum(
        "brckj,brckl->kjl", hidden_blocks, up_back, preferred_element_type=jnp.float32
    )
    hidden_grad = (
        upstream
        + jnp.einsum("brckl,kjl->brckj", gate_back, blocks_gate, preferred_element_type=jnp.float32)
        + jnp.einsum("brckl,kjl->brckj", up_back, blocks_up, preferred_element_type=jnp.float32)
    )
    hidden_grad = hidden_grad.reshape(inputs.shape).astype(jnp.bfloat16)
    segment = lax.all_to_all(hidden_grad, "seq", split_axis=2, concat_axis=1, tiled=True)
    mixed = jnp.einsum(
        "er,becd->brcd", cols_mix, segment, preferred_element_type=jnp.float32
    ).astype(jnp.bfloat16)
    cols_sum = jnp.einsum("becd,brcd->er", segment, first_cols, preferred_element_type=jnp.float32)
    first_grad = lax.all_to_all(mixed, "seq", split_axis=1, concat_axis=2, tiled=True)
    rows_sum = jnp.einsum("bred,brcd->ec", first_grad, inputs, preferred_element_type=jnp.float32)
    input_grad = (
        hidden_grad.astype(jnp.float32)
        + jnp.einsum("ec,bred->brcd", rows_in, first_grad, preferred_element_type=jnp.float32)
    ).astype(jnp.bfloat16)
    rows_total, cols_total = lax.psum((rows_sum, cols_sum), ("dp", "seq", "chan"))
    gate_blocks_total, up_blocks_total, gate_mix_total, up_mix_total = lax.psum(
        (blocks_gate_sum, blocks_up_sum, mix_gate_sum, mix_up_sum), ("dp", "seq")
    )
    count_dp = lax.axis_size("dp")
    count_seq = lax.axis_size("seq")
    count_chan = lax.axis_size("chan")
    batch_all = batch_dev * count_dp
    rows_all = rows_dev * count_seq
    width_all = width_dev * count_chan
    rows_scale = 1.0 / math.sqrt(batch_all * rows_all * width_all)
    cols_scale = 1.0 / math.sqrt(batch_all * cols_all * width_all)
    block_scale = 1.0 / math.sqrt(batch_all * rows_all * cols_all)
    return (
        input_grad,
        rows_total * rows_scale,
        cols_total * cols_scale,
        gate_blocks_total * block_scale,
        up_blocks_total * block_scale,
        gate_mix_total * block_scale,
        up_mix_total * block_scale,
    )


def solution(mesh):
    in_specs = (
        P("dp", "seq", None, "chan"),
        P("dp", "seq", None, "chan"),
        P(),
        P(),
        P("chan", None, None),
        P("chan", None, None),
        P(),
        P(),
    )
    out_specs = (
        P("dp", "seq", None, "chan"),
        P(),
        P(),
        P("chan", None, None),
        P("chan", None, None),
        P(None, "chan", None),
        P(None, "chan", None),
    )
    sizes = dict(mesh.shape)
    fits = sizes["dp"] == 4 and sizes["seq"] == 4 and sizes["chan"] == 2
    return jax.shard_map(block_body if fits else body, mesh=mesh, in_specs=in_specs, out_specs=out_specs, check_vma=False)
```

```python
import functools
import math

import jax
import jax.numpy as jnp
from jax import lax
from jax.experimental import pallas as pl
from jax.experimental.pallas import tpu as pltpu
from jax.sharding import PartitionSpec as P

BF = jnp.bfloat16
F = jnp.float32
VM = pl.BlockSpec(memory_space=pltpu.VMEM)
SM = pl.BlockSpec(memory_space=pltpu.SMEM)
PARAMS = pltpu.CompilerParams(vmem_limit_bytes=20 * 1024 * 1024)


def whole(*dims):
    return pl.BlockSpec(dims, lambda j: (0,) * len(dims))


def wholes(*values):
    return [whole(*value.shape) for value in values]


def once(kernel):
    def run(*refs):
        @pl.when(pl.program_id(0) == 0)
        def _():
            kernel(*refs)

    return run


def held_in_hbm(*values):
    return [pltpu.with_memory_space_constraint(value, pltpu.HBM) for value in values]


def shape_of(dims, kind=BF):
    return pltpu.HBM(dims, kind)


def turned_blocks(table, at, step, n, rows, axis):
    return jnp.concatenate(
        [
            lax.dynamic_slice_in_dim(table, lax.rem(at + n + step * j, n) * rows, rows, axis)
            for j in range(n)
        ],
        axis=axis,
    )


def mix_tables(mix, at, n, rows, cw):
    size = mix.shape[0]
    same = lax.broadcasted_iota(jnp.int32, (1, cw, 1, cw), 1) == lax.broadcasted_iota(
        jnp.int32, (1, cw, 1, cw), 3
    )

    def spread(table):
        grown = jnp.where(same, table[:, None, :, None], jnp.zeros((), BF))
        return grown.reshape(size * cw, size * cw)

    ahead = turned_blocks(turned_blocks(mix, at, -1, n, rows, 1), at, 1, n, rows, 0)
    back = mix.T.reshape(n, rows, n, rows).transpose(1, 0, 3, 2).reshape(size, size)
    return spread(ahead), spread(back)


def column_mix_kernel(count, table, *refs):
    sources, outs = refs[:count], refs[count:]
    whole_source = jnp.concatenate([source[...] for source in sources], axis=0)
    total = jnp.dot(table[...], whole_source, preferred_element_type=F).astype(BF)
    deep = outs[0].shape[0]
    for i, out in enumerate(outs):
        out[...] = total[i * deep : (i + 1) * deep]


def column_mix(table, sources, outs, name):
    size = table.shape[0]
    width = sources[0].shape[-1]
    lanes = 512
    deep = size // outs
    return pl.pallas_call(
        functools.partial(column_mix_kernel, len(sources)),
        out_shape=[shape_of((deep, width))] * outs,
        grid=(width // lanes,),
        in_specs=[pl.BlockSpec((size, size), lambda j: (0, 0))]
        + [pl.BlockSpec((source.shape[0], lanes), lambda j: (0, j)) for source in sources],
        out_specs=[pl.BlockSpec((deep, lanes), lambda j: (0, j))] * outs,
        name=name,
    )(*held_in_hbm(table), *sources)


def column_sum_kernel(cw, rows, *refs):
    pieces, sources, (out, left, right) = refs[:rows], refs[rows:-3], refs[-3:]
    for side, parts in ((left, pieces), (right, sources)):
        deep = parts[0].shape[0]
        for j, part in enumerate(parts):
            side[j * deep : (j + 1) * deep, :] = part[...]
    product = lax.dot_general(
        left[...], right[...], (((1,), (1,)), ((), ())), preferred_element_type=F
    )
    size = product.shape[0]
    row_at = lax.broadcasted_iota(jnp.int32, (size, size), 0)
    col_at = lax.broadcasted_iota(jnp.int32, (size, size), 1)
    kept = jnp.where(lax.rem(row_at, cw) == lax.rem(col_at, cw), product, 0.0)
    out[...] = jnp.sum(kept.reshape(size // cw, cw, size), axis=1)


def column_sum(cw, sources, pieces):
    width = pieces[0].shape[1]
    size = sum(piece.shape[0] for piece in pieces)
    return pl.pallas_call(
        once(functools.partial(column_sum_kernel, cw, len(pieces))),
        out_shape=shape_of((size // cw, size), F),
        grid=(2,),
        in_specs=wholes(*pieces, *sources),
        out_specs=whole(size // cw, size),
        scratch_shapes=[pltpu.VMEM((size, width), BF)] * 2,
        compiler_params=PARAMS,
        name="column_sum",
    )(*held_in_hbm(*pieces, *sources))


def hidden_kernel(n, place, rows_in, x, own, *refs):
    received, (hidden, mixed) = refs[: n - 1], refs[n - 1 :]
    cw, lanes = own.shape
    side = pl.ds(pl.multiple_of(pl.program_id(0) * lanes, lanes), lanes)
    for i in range(n):
        spot = pl.multiple_of(lax.rem(place[0] + n - i, n) * cw, cw)
        mixed[pl.ds(spot, cw), :] = own[...] if i == 0 else received[i - 1][:, side]
    second = jnp.dot(rows_in[...], mixed[...], preferred_element_type=F)
    hidden[...] = (x[...].astype(F) + second).astype(BF)


def hidden_row(place, rows_in, inputs, h, pieces):
    cols, width = inputs.shape[1:]
    n = len(pieces)
    lanes = 512
    column = pl.BlockSpec((cols, lanes), lambda j: (0, j))
    return pl.pallas_call(
        functools.partial(hidden_kernel, n),
        out_shape=[shape_of((cols, width))] * 2,
        grid=(width // lanes,),
        in_specs=[
            SM,
            pl.BlockSpec((cols, cols), lambda j: (0, 0)),
            pl.BlockSpec((None, cols, lanes), lambda j: (h, 0, j)),
            pl.BlockSpec((cols // n, lanes), lambda j: (0, j)),
        ]
        + [VM] * (n - 1),
        out_specs=[column, column],
        name="hidden_row",
    )(place, *held_in_hbm(rows_in, inputs, pieces[0]), *pieces[1:])


def channel_kernel(first, *refs):
    (place, h_own, h_oth, c_own, c_oth, wg_own, wu_own, *lent) = refs[:11]
    mix_g, mix_u, rows_in, mixed, *before = refs[11 : 15 if first else 16]
    hid_grad, back_g, back_u, turned, mix_sum, row_sum, mid = refs[-7:]
    mid_g, mid_u = mid.at[0], mid.at[1]
    local, size = wg_own.shape[:2]
    blocks = 2 * local
    cols = h_own.shape[0]
    for k in range(local):
        part = h_own[:, k * size : (k + 1) * size]
        mid_g[k] = jnp.dot(part, wg_own[k], preferred_element_type=F)
        mid_u[k] = jnp.dot(part, wu_own[k], preferred_element_type=F)
    core, x = place[2], place[3]
    for i, block in enumerate(lent):
        table = core if i < 2 else 1 - core
        k = x if i % 2 == 0 else 1 - x
        part = h_oth[:, pl.ds(pl.multiple_of(k * size, size), size)]
        mid[table, local + k] = jnp.dot(part, block[...], preferred_element_type=F)
    mix_sum[...] = jnp.zeros_like(mix_sum)
    deep, lanes = 16, 128

    def chunk(t, carry):
        rows = pl.ds(pl.multiple_of(t * deep, deep), deep)
        for q in range(size // lanes):
            at = slice(q * lanes, (q + 1) * lanes)
            shape = (deep // 8, 8, lanes)
            g = [mid_g[k, rows, at].reshape(shape) for k in range(blocks)]
            u = [mid_u[k, rows, at].reshape(shape) for k in range(blocks)]
            sum_g, sum_u = [None] * local, [None] * local
            for m in range(blocks):
                c = c_own if m < local else c_oth
                start = (m % local) * size + q * lanes
                up = c[rows, start : start + lanes].astype(F).reshape(shape)
                gate_out = mix_g[m, 0, :, at] * g[0]
                up_out = mix_u[m, 0, :, at] * u[0]
                for k in range(1, blocks):
                    gate_out = gate_out + mix_g[m, k, :, at] * g[k]
                    up_out = up_out + mix_u[m, k, :, at] * u[k]
                sigma = 0.5 * jnp.tanh(0.5 * gate_out) + 0.5
                scaled = up * sigma
                up_grad = scaled * gate_out
                gate_grad = scaled * up_out * (1.0 + gate_out * (1.0 - sigma))
                for k in range(local):
                    mix_sum[0, m, k, :, at] += jnp.sum(gate_grad * g[k], axis=0)
                    mix_sum[1, m, k, :, at] += jnp.sum(up_grad * u[k], axis=0)
                    term_g = mix_g[m, k, :, at] * gate_grad
                    term_u = mix_u[m, k, :, at] * up_grad
                    sum_g[k] = term_g if m == 0 else sum_g[k] + term_g
                    sum_u[k] = term_u if m == 0 else sum_u[k] + term_u
            for k in range(local):
                spot = slice(k * size + q * lanes, k * size + (q + 1) * lanes)
                back_g[rows, spot] = sum_g[k].reshape(deep, lanes).astype(BF)
                back_u[rows, spot] = sum_u[k].reshape(deep, lanes).astype(BF)
        return carry

    lax.fori_loop(0, cols // deep, chunk, 0)
    last = (((1,), (1,)), ((), ()))
    for k in range(local):
        spot = slice(k * size, (k + 1) * size)
        grad = lax.dot_general(back_g[:, spot], wg_own[k], last, preferred_element_type=F)
        grad = grad + lax.dot_general(back_u[:, spot], wu_own[k], last, preferred_element_type=F)
        hid_grad[:, spot] = (c_own[:, spot].astype(F) + grad).astype(BF)
    turned[...] = lax.dot_general(
        rows_in[...], hid_grad[...], (((0,), (0,)), ((), ())), preferred_element_type=F
    ).astype(BF)
    total = lax.dot_general(hid_grad[...], mixed[...], last, preferred_element_type=F)
    for held in before:
        total = held[...] + total
    row_sum[...] = total


def channel_row(place, h, h_own, h_oth, cot, cot_oth, weights, mixes, rows_in, mixed, before):
    cols, width = h_own.shape
    local, size = weights[0].shape[:2]
    blocks = 2 * local
    row = pl.BlockSpec((None, cols, width), lambda j: (h, 0, 0))
    return pl.pallas_call(
        once(functools.partial(channel_kernel, not before)),
        out_shape=[shape_of((cols, width))] * 4
        + [shape_of((2, blocks, local, 8, size), F), shape_of((cols, cols), F)],
        grid=(2,),
        in_specs=[SM]
        + wholes(h_own, h_oth)
        + [row, row]
        + [VM] * 2
        + wholes(*weights[2:], *mixes, rows_in, mixed, *before),
        out_specs=[whole(cols, width)] * 4
        + [whole(2, blocks, local, 8, size), whole(cols, cols)],
        scratch_shapes=[pltpu.VMEM((2, blocks, cols, size), F)],
        compiler_params=PARAMS,
        name="channel_row",
    )(
        place,
        *held_in_hbm(h_own, h_oth, cot, cot_oth),
        *weights[:2],
        *held_in_hbm(*weights[2:], *mixes, rows_in, mixed, *before),
    )


def sums_kernel(rows, parts, place, row_sum, *refs):
    hid, back_g, back_u, mix_sum = (refs[i * rows : (i + 1) * rows] for i in range(4))
    outs = refs[4 * rows :]
    size = outs[0].shape[-1]
    local = hid[0].shape[1] // size
    blocks = 2 * local
    first = (((0,), (0,)), ((), ()))
    high = local * size // parts
    per = size // high
    chan, core = place[1], place[2]
    for part, out in ((1, outs[1]), (0, outs[0])):
        k = core if part == 0 else 1 - core
        spot = pl.ds(pl.multiple_of(k * size, size), size)
        for w, back in enumerate((back_g, back_u)):
            total = None
            for h in range(rows):
                term = lax.dot_general(
                    hid[h][:, spot], back[h][:, spot], first, preferred_element_type=F
                )
                total = term if total is None else total + term
            for q in range(per):
                out[q, w * high : (w + 1) * high, :] = total[q * high : (q + 1) * high].astype(BF)
        for q in range(per):
            p = k * per + q
            m_at = lax.rem(p // (2 * local) + blocks - chan * local, blocks)
            k_at = lax.rem(p // 2, local)
            lines = [
                jnp.sum(sum(ref[w, m_at, k_at] for ref in mix_sum), axis=0, keepdims=True)
                for w in range(2)
            ]
            at = pl.multiple_of(p * 16, 16)
            eight = jnp.concatenate(
                [row_sum[pl.ds(at, 8), :], row_sum[pl.ds(at + 8, 8), :]], axis=1
            )
            tail = jnp.concatenate([eight, *lines, jnp.zeros((6, size), F)], axis=0)
            out[q, 2 * high :, :] = tail.astype(BF)


def sums(place, parts, row_sum, hid, back_g, back_u, mix_sum):
    rows = len(hid)
    size = mix_sum[0].shape[-1]
    high = hid[0].shape[1] // parts
    dims = (parts // 2, 2 * high + 16, size)
    return pl.pallas_call(
        once(functools.partial(sums_kernel, rows, parts)),
        out_shape=[shape_of(dims)] * 2,
        grid=(2,),
        in_specs=[SM] + wholes(row_sum, *hid, *back_g, *back_u, *mix_sum),
        out_specs=[whole(*dims)] * 2,
        compiler_params=PARAMS,
        name="sums",
    )(place, *held_in_hbm(row_sum, *hid, *back_g, *back_u, *mix_sum))


def core_add_kernel(n, place, kept, got, *outs):
    at, x = place[0], place[3]
    for i in range(n):
        for part in range(2):
            q = (x if part else 1 - x) * n + lax.rem(at + i, n)
            out = outs[n].at[i] if part else outs[i]
            out[...] = (kept[q].astype(F) + got[q].astype(F)).astype(BF)


def core_add(n, place, kept, got):
    deep, size = kept.shape[1:]
    return pl.pallas_call(
        once(functools.partial(core_add_kernel, n)),
        out_shape=[shape_of((deep, size))] * n + [shape_of((n, deep, size))],
        grid=(2,),
        in_specs=[SM] + wholes(kept, got),
        out_specs=[whole(deep, size)] * n + [whole(n, deep, size)],
        compiler_params=PARAMS,
        name="core_add",
    )(place, *held_in_hbm(kept), got)


def unpack_kernel(n, scales, place, *refs):
    held = refs[:4]
    gate, up, rows, mix_g, mix_u, cols_out, lines = refs[4:]
    local = mix_g.shape[1]
    at, core, x = place[0], place[2], place[3]
    high = gate.shape[0] // (4 * n)
    half = rows.shape[1]
    for i in range(4):
        base = lax.rem(core + i // 2, 2) * 2 * n + lax.rem(x + i % 2, 2) * n
        for j in range(n):
            p = base + lax.rem(at + n - j, n)
            spot = pl.ds(pl.multiple_of(p * high, high), high)
            gate[spot, :] = held[i][j, :high, :].astype(F) * scales[1]
            up[spot, :] = held[i][j, high : 2 * high, :].astype(F) * scales[1]
            tail = held[i][j, 2 * high :, :].astype(F)
            where = pl.multiple_of(p * 16, 16)
            rows[pl.ds(where, 8), :] = tail[:8, :half] * scales[0]
            rows[pl.ds(where + 8, 8), :] = tail[:8, half:] * scales[0]
            for w, out in enumerate((mix_g, mix_u)):
                spot = (pl.ds(p // (2 * local), 1), pl.ds(lax.rem(p // 2, local), 1), slice(None))
                out[spot] = tail[None, 8 + w : 9 + w, :] * scales[1]
            lines[pl.ds(p, 1), :] = tail[10:11, :] + tail[11:12, :]
    total = jnp.sum(lines[...], axis=0, keepdims=True) * scales[2]
    count = cols_out.shape[0]
    for r in range(count):
        cols_out[r : r + 1, :] = total[:, r * count : (r + 1) * count]


def unpack(n, rows, local, scales, place, held, cols):
    deep, size = held[0].shape[1:]
    high = (deep - 16) // 2
    return pl.pallas_call(
        functools.partial(unpack_kernel, n, scales),
        out_shape=[shape_of((4 * n * high, size), F)] * 2
        + [shape_of((cols, cols), F)]
        + [shape_of((2 * local, local, size), F)] * 2
        + [shape_of((n * rows, n * rows), F)],
        grid=(1,),
        in_specs=[SM] + wholes(*held),
        out_specs=[whole(4 * n * high, size)] * 2
        + [whole(cols, cols)]
        + [whole(2 * local, local, size)] * 2
        + [whole(n * rows, n * rows)],
        scratch_shapes=[pltpu.VMEM((4 * n, size), F)],
        compiler_params=PARAMS,
        name="unpack",
    )(place, *held)


def finish_kernel(grad, back, *refs):
    lanes = grad.shape[1]
    side = pl.ds(pl.multiple_of(pl.program_id(0) * lanes, lanes), lanes)
    refs[-1][...] = (grad[...].astype(F) + back[:, side].astype(F)).astype(BF)


def finish(h, rows, grad, back, before):
    cols, width = grad.shape
    lanes = 512
    return pl.pallas_call(
        finish_kernel,
        out_shape=shape_of((rows, cols, width)),
        grid=(width // lanes,),
        in_specs=[pl.BlockSpec((cols, lanes), lambda j: (0, j)), VM]
        + [pl.BlockSpec(memory_space=pltpu.HBM)] * len(before),
        out_specs=pl.BlockSpec((None, cols, lanes), lambda j: (h, 0, j)),
        input_output_aliases={2: 0} if before else {},
        name="finish",
    )(*held_in_hbm(grad), back, *before)


def shifted(value, by, n):
    return lax.ppermute(value, "seq", [(i, (i + by) % n) for i in range(n)])


def swapped(value, axis, bit, n):
    return lax.ppermute(value, axis, [(i, i ^ bit) for i in range(n)])


def traded(value):
    return lax.all_to_all(value, "seq", split_axis=0, concat_axis=0, tiled=True)


def pick(value, index):
    return lax.dynamic_index_in_dim(value, index, 0, keepdims=False)


def add(*values):
    return sum(value.astype(F) for value in values).astype(BF)


def two_lines(line):
    upper = line.astype(BF)
    return upper, (line - upper.astype(F)).astype(BF)


def two_lines(line):
    upper = line.astype(BF)
    return upper, (line - upper.astype(F)).astype(BF)


def scatter_seq(by_x, fours, cols_sum, n):
    deep, size = fours.shape[1:]
    arrived = []
    for i in [*range(1, n), 0]:
        shard = add(fours[i], by_x[i])
        arrived.append(shifted(shard, i, n) if i else shard)
    count = cols_sum.size
    line = jnp.pad(cols_sum.reshape(1, count), ((0, 0), (0, size - count)))
    lines = jnp.pad(jnp.concatenate(two_lines(line), axis=0), ((deep - 6, 4), (0, 0)))
    mine = add(*arrived, lines)
    tail = mine[deep - 16 :]
    other = swapped(tail, "chan", 1, 2)
    both = tail.astype(F) + other.astype(F)
    lines = two_lines(both[10:11] + both[11:12])
    tail = jnp.concatenate([both[:8].astype(BF), tail[8:10], *lines, tail[12:]], axis=0)
    return jnp.concatenate([mine[: deep - 16], tail], axis=0)


def block_body(inputs, cotangent, rows_in, cols_mix, blocks_gate, blocks_up, mix_gate, mix_up):
    n = lax.axis_size("seq")
    rows, cols, width = inputs.shape[1:]
    local, size = blocks_gate.shape[:2]
    cw = cols // n
    seq_at, chan_at, dp_at = lax.axis_index("seq"), lax.axis_index("chan"), lax.axis_index("dp")
    core, x = lax.rem(dp_at, 2), dp_at // 2
    place = jnp.stack([seq_at, chan_at, core, x]).astype(jnp.int32)
    values, cot = inputs[0], cotangent[0]
    ahead, behind = mix_tables(cols_mix, seq_at, n, rows, cw)

    def relative(table):
        turned = jnp.roll(table, (local, local), (0, 1))
        table = jnp.where(chan_at == 0, table, turned).astype(F)
        return jnp.broadcast_to(table[:, :, None, :], table.shape[:2] + (8, size))

    ways = [
        lax.dynamic_slice_in_dim(values, lax.rem(seq_at + i, n) * cw, cw, 1) for i in range(n)
    ]
    x_cols = [ways[0]] + [shifted(ways[i], i, n) for i in range(1, n)]
    x_cols = [part.reshape(rows * cw, width) for part in x_cols]
    lent = pick(jnp.where(core == 0, blocks_gate, blocks_up), x)
    lent = swapped(lent, "chan", 1, 2)
    leaving, _ = lax.optimization_barrier((cot, lent))
    cot_oth = swapped(leaving, "chan", 1, 2)
    lent = [lent, swapped(lent, "dp", 2, 4)]
    mixes = (relative(mix_gate), relative(mix_up))

    x_cols, ahead, behind, mixes = lax.optimization_barrier((x_cols, ahead, behind, mixes))
    parts = column_mix(ahead, x_cols, n * rows, "column_mix")
    parts, lent = lax.optimization_barrier((parts, lent))
    passed = [swapped(block, "dp", 1, 4) for block in lent]
    parts = list(parts)
    held_up = [i for i in range(n * rows) if i not in (0, rows, 2 * rows)]
    late, passed = lax.optimization_barrier(([parts[i] for i in held_up], passed))
    for i, part in zip(held_up, late):
        parts[i] = part
    lent = lent + passed
    got = [
        [parts[h]] + [shifted(parts[i * rows + h], i, n) for i in range(1, n)]
        for h in range(rows)
    ]
    got[0], cot_oth = lax.optimization_barrier((got[0], cot_oth))
    hidden, mixed = [], []
    for h in range(rows):
        for held, value in zip((hidden, mixed), hidden_row(place, rows_in, values, h, got[h])):
            held.append(value)
    weights = (blocks_gate, blocks_up, *lent)
    others = [swapped(hid, "chan", 1, 2) for hid in hidden]
    others[0], hidden[-1] = lax.optimization_barrier((others[0], hidden[-1]))
    grads, back_g, back_u, pieces, mix_sum, rows_sum = [], [], [], [], [], []
    for h in range(rows):
        got = channel_row(
            place,
            h,
            hidden[h],
            others[h],
            cot,
            cot_oth,
            weights,
            mixes,
            rows_in,
            mixed[h],
            rows_sum,
        )
        for held, value in zip((grads, back_g, back_u, pieces, mix_sum), got):
            held.append(value)
        rows_sum = got[5:]
    kept, sent = sums(place, 4 * n, rows_sum[0], hidden, back_g, back_u, mix_sum)
    pieces[0], _ = lax.optimization_barrier((pieces[0], others[-1]))
    pieces[0] = traded(pieces[0].reshape(n, cw, width)).reshape(cols, width)
    sent, _ = lax.optimization_barrier((sent, pieces[0]))
    pieces[1], _ = lax.optimization_barrier((pieces[1], kept))
    pieces[1] = traded(pieces[1].reshape(n, cw, width)).reshape(cols, width)
    *leaving, fours = core_add(n, place, kept, swapped(sent, "dp", 1, 4))
    by_x = [swapped(shard, "dp", 2, 4) for shard in leaving]
    pieces[1], _ = lax.optimization_barrier((pieces[1], by_x[1]))
    turned = column_mix(behind, pieces, rows, "column_back")
    backs = [traded(turned[0].reshape(n, cw, width))]
    late, _ = lax.optimization_barrier((pieces[1], turned[0]))
    cols_sum = column_sum(cw, x_cols, [pieces[0], late])
    cols_sum = cols_sum.reshape(rows, n, n * rows, cw).sum(-1).transpose(1, 0, 2)
    cols_sum = turned_blocks(cols_sum.reshape(n * rows, n * rows), seq_at, -1, n, rows, 1)
    mine = scatter_seq(by_x, fours, cols_sum, n)
    held = [mine] + [shifted(mine, i, n) for i in range(1, n)]
    for part in turned[1:]:
        part, _ = lax.optimization_barrier((part, held[1]))
        backs.append(traded(part.reshape(n, cw, width)))
    backs = [part.reshape(cols, width) for part in backs]
    batch_all = lax.axis_size("dp")
    width_all = width * lax.axis_size("chan")
    rows_scale = 1.0 / math.sqrt(batch_all * rows * n * width_all)
    cols_scale = 1.0 / math.sqrt(batch_all * cols * width_all)
    block_scale = 1.0 / math.sqrt(batch_all * rows * n * cols)
    by_x = jnp.stack([swapped(shard, "dp", 2, 4) for shard in held])
    held = jnp.stack(held)
    by_core = swapped(held, "dp", 1, 4)
    done = []
    for h in range(rows):
        done = [finish(h, rows, grads[h], backs[h], done)]
    input_grad = done[0]
    gate_sum, up_sum, rows_sum, mix_g, mix_u, cols_sum = unpack(
        n,
        rows,
        local,
        (rows_scale, block_scale, cols_scale),
        place,
        (held, by_x, by_core, swapped(by_x, "dp", 1, 4)),
        cols,
    )
    return (
        input_grad[None],
        rows_sum,
        cols_sum,
        gate_sum.reshape(local, size, size),
        up_sum.reshape(local, size, size),
        mix_g,
        mix_u,
    )


def column_keep(segment, cols_mix):
    mixed = jnp.einsum(
        "er,brcd->becd", cols_mix, segment, preferred_element_type=jnp.float32
    ).astype(jnp.bfloat16)
    return (segment, mixed)

def body(inputs, cotangent, rows_in, cols_mix, blocks_gate, blocks_up, mix_gate, mix_up):
    batch_dev, rows_dev, cols_all, width_dev = inputs.shape
    block_size = blocks_gate.shape[1]
    local_blocks = blocks_gate.shape[0]
    chan_index = lax.axis_index("chan")
    split_shape = (batch_dev, rows_dev, cols_all, local_blocks, block_size)
    first = jnp.einsum("ec,brcd->bred", rows_in, inputs, preferred_element_type=jnp.float32).astype(
        jnp.bfloat16
    )
    first_cols, second_cols = column_keep(
        lax.all_to_all(first, "seq", split_axis=2, concat_axis=1, tiled=True), cols_mix
    )
    second_rows = lax.all_to_all(second_cols, "seq", split_axis=1, concat_axis=2, tiled=True)
    hidden = (inputs.astype(jnp.float32) + second_rows.astype(jnp.float32)).astype(jnp.bfloat16)
    hidden_blocks = hidden.reshape(split_shape)
    gate_rows_own = lax.dynamic_slice_in_dim(
        mix_gate, chan_index * local_blocks, local_blocks, 0
    ).astype(jnp.float32)
    up_rows_own = lax.dynamic_slice_in_dim(
        mix_up, chan_index * local_blocks, local_blocks, 0
    ).astype(jnp.float32)
    gate_mid = jnp.einsum(
        "brckj,kjl->brckl", hidden_blocks, blocks_gate, preferred_element_type=jnp.float32
    ).astype(jnp.bfloat16)
    up_mid = jnp.einsum(
        "brckj,kjl->brckl", hidden_blocks, blocks_up, preferred_element_type=jnp.float32
    ).astype(jnp.bfloat16)
    gate_add = jnp.einsum(
        "mkj,brckj->brcmj",
        gate_rows_own,
        lax.all_gather(gate_mid, "chan", axis=3, tiled=True).astype(jnp.float32),
    )
    up_add = jnp.einsum(
        "mkj,brckj->brcmj",
        up_rows_own,
        lax.all_gather(up_mid, "chan", axis=3, tiled=True).astype(jnp.float32),
    )
    upstream = cotangent.astype(jnp.float32).reshape(split_shape)
    sigma = jax.nn.sigmoid(gate_add)
    up_grad = (upstream * gate_add * sigma).astype(jnp.bfloat16)
    gate_grad = (upstream * up_add * sigma * (1.0 + gate_add * (1.0 - sigma))).astype(jnp.bfloat16)
    gate_all, up_all = (
        lax.all_gather(gate_grad, "chan", axis=3, tiled=True),
        lax.all_gather(up_grad, "chan", axis=3, tiled=True),
    )
    gate_cols_own = lax.dynamic_slice_in_dim(
        mix_gate, chan_index * local_blocks, local_blocks, 1
    ).astype(jnp.float32)
    up_cols_own = lax.dynamic_slice_in_dim(
        mix_up, chan_index * local_blocks, local_blocks, 1
    ).astype(jnp.float32)
    mix_gate_sum = jnp.einsum(
        "brcmj,brckj->mkj", gate_all, gate_mid, preferred_element_type=jnp.float32
    )
    mix_up_sum = jnp.einsum("brcmj,brckj->mkj", up_all, up_mid, preferred_element_type=jnp.float32)
    gate_back = jnp.einsum("mkj,brcmj->brckj", gate_cols_own, gate_all.astype(jnp.float32)).astype(
        jnp.bfloat16
    )
    up_back = jnp.einsum("mkj,brcmj->brckj", up_cols_own, up_all.astype(jnp.float32)).astype(
        jnp.bfloat16
    )
    blocks_gate_sum = jnp.einsum(
        "brckj,brckl->kjl", hidden_blocks, gate_back, preferred_element_type=jnp.float32
    )
    blocks_up_sum = jnp.einsum(
        "brckj,brckl->kjl", hidden_blocks, up_back, preferred_element_type=jnp.float32
    )
    hidden_grad = (
        upstream
        + jnp.einsum("brckl,kjl->brckj", gate_back, blocks_gate, preferred_element_type=jnp.float32)
        + jnp.einsum("brckl,kjl->brckj", up_back, blocks_up, preferred_element_type=jnp.float32)
    )
    hidden_grad = hidden_grad.reshape(inputs.shape).astype(jnp.bfloat16)
    segment = lax.all_to_all(hidden_grad, "seq", split_axis=2, concat_axis=1, tiled=True)
    mixed = jnp.einsum(
        "er,becd->brcd", cols_mix, segment, preferred_element_type=jnp.float32
    ).astype(jnp.bfloat16)
    cols_sum = jnp.einsum("becd,brcd->er", segment, first_cols, preferred_element_type=jnp.float32)
    first_grad = lax.all_to_all(mixed, "seq", split_axis=1, concat_axis=2, tiled=True)
    rows_sum = jnp.einsum("bred,brcd->ec", first_grad, inputs, preferred_element_type=jnp.float32)
    input_grad = (
        hidden_grad.astype(jnp.float32)
        + jnp.einsum("ec,bred->brcd", rows_in, first_grad, preferred_element_type=jnp.float32)
    ).astype(jnp.bfloat16)
    rows_total, cols_total = lax.psum((rows_sum, cols_sum), ("dp", "seq", "chan"))
    gate_blocks_total, up_blocks_total, gate_mix_total, up_mix_total = lax.psum(
        (blocks_gate_sum, blocks_up_sum, mix_gate_sum, mix_up_sum), ("dp", "seq")
    )
    count_dp = lax.axis_size("dp")
    count_seq = lax.axis_size("seq")
    count_chan = lax.axis_size("chan")
    batch_all = batch_dev * count_dp
    rows_all = rows_dev * count_seq
    width_all = width_dev * count_chan
    rows_scale = 1.0 / math.sqrt(batch_all * rows_all * width_all)
    cols_scale = 1.0 / math.sqrt(batch_all * cols_all * width_all)
    block_scale = 1.0 / math.sqrt(batch_all * rows_all * cols_all)
    return (
        input_grad,
        rows_total * rows_scale,
        cols_total * cols_scale,
        gate_blocks_total * block_scale,
        up_blocks_total * block_scale,
        gate_mix_total * block_scale,
        up_mix_total * block_scale,
    )


def solution(mesh):
    in_specs = (
        P("dp", "seq", None, "chan"),
        P("dp", "seq", None, "chan"),
        P(),
        P(),
        P("chan", None, None),
        P("chan", None, None),
        P(),
        P(),
    )
    out_specs = (
        P("dp", "seq", None, "chan"),
        P(),
        P(),
        P("chan", None, None),
        P("chan", None, None),
        P(None, "chan", None),
        P(None, "chan", None),
    )
    sizes = dict(mesh.shape)
    fits = sizes["dp"] == 4 and sizes["seq"] == 4 and sizes["chan"] == 2
    return jax.shard_map(block_body if fits else body, mesh=mesh, in_specs=in_specs, out_specs=out_specs, check_vma=False)
```

```python
import functools
import math

import jax
import jax.numpy as jnp
from jax import lax
from jax.experimental import pallas as pl
from jax.experimental.pallas import tpu as pltpu
from jax.sharding import PartitionSpec as P

BF = jnp.bfloat16
F = jnp.float32
VM = pl.BlockSpec(memory_space=pltpu.VMEM)
SM = pl.BlockSpec(memory_space=pltpu.SMEM)
PARAMS = pltpu.CompilerParams(vmem_limit_bytes=20 * 1024 * 1024)


def whole(*dims):
    return pl.BlockSpec(dims, lambda j: (0,) * len(dims))


def wholes(*values):
    return [whole(*value.shape) for value in values]


def once(kernel):
    def run(*refs):
        @pl.when(pl.program_id(0) == 0)
        def _():
            kernel(*refs)

    return run


def held_in_hbm(*values):
    return [pltpu.with_memory_space_constraint(value, pltpu.HBM) for value in values]


def shape_of(dims, kind=BF):
    return pltpu.HBM(dims, kind)


def turned_blocks(table, at, step, n, rows, axis):
    return jnp.concatenate(
        [
            lax.dynamic_slice_in_dim(table, lax.rem(at + n + step * j, n) * rows, rows, axis)
            for j in range(n)
        ],
        axis=axis,
    )


def mix_tables(mix, at, n, rows, cw):
    size = mix.shape[0]
    same = lax.broadcasted_iota(jnp.int32, (1, cw, 1, cw), 1) == lax.broadcasted_iota(
        jnp.int32, (1, cw, 1, cw), 3
    )

    def spread(table):
        grown = jnp.where(same, table[:, None, :, None], jnp.zeros((), BF))
        return grown.reshape(size * cw, size * cw)

    ahead = turned_blocks(turned_blocks(mix, at, -1, n, rows, 1), at, 1, n, rows, 0)
    back = mix.T.reshape(n, rows, n, rows).transpose(1, 0, 3, 2).reshape(size, size)
    return spread(ahead), spread(back)


def column_mix_kernel(count, table, *refs):
    sources, outs = refs[:count], refs[count:]
    whole_source = jnp.concatenate([source[...] for source in sources], axis=0)
    total = jnp.dot(table[...], whole_source, preferred_element_type=F).astype(BF)
    deep = outs[0].shape[0]
    for i, out in enumerate(outs):
        out[...] = total[i * deep : (i + 1) * deep]


def column_mix(table, sources, outs, name):
    size = table.shape[0]
    width = sources[0].shape[-1]
    lanes = 512
    deep = size // outs
    return pl.pallas_call(
        functools.partial(column_mix_kernel, len(sources)),
        out_shape=[shape_of((deep, width))] * outs,
        grid=(width // lanes,),
        in_specs=[pl.BlockSpec((size, size), lambda j: (0, 0))]
        + [pl.BlockSpec((source.shape[0], lanes), lambda j: (0, j)) for source in sources],
        out_specs=[pl.BlockSpec((deep, lanes), lambda j: (0, j))] * outs,
        name=name,
    )(*held_in_hbm(table), *sources)


def column_sum_kernel(cw, rows, *refs):
    pieces, sources, (out, left, right) = refs[:rows], refs[rows:-3], refs[-3:]
    for side, parts in ((left, pieces), (right, sources)):
        deep = parts[0].shape[0]
        for j, part in enumerate(parts):
            side[j * deep : (j + 1) * deep, :] = part[...]
    product = lax.dot_general(
        left[...], right[...], (((1,), (1,)), ((), ())), preferred_element_type=F
    )
    size = product.shape[0]
    row_at = lax.broadcasted_iota(jnp.int32, (size, size), 0)
    col_at = lax.broadcasted_iota(jnp.int32, (size, size), 1)
    kept = jnp.where(lax.rem(row_at, cw) == lax.rem(col_at, cw), product, 0.0)
    out[...] = jnp.sum(kept.reshape(size // cw, cw, size), axis=1)


def column_sum(cw, sources, pieces):
    width = pieces[0].shape[1]
    size = sum(piece.shape[0] for piece in pieces)
    return pl.pallas_call(
        once(functools.partial(column_sum_kernel, cw, len(pieces))),
        out_shape=shape_of((size // cw, size), F),
        grid=(2,),
        in_specs=wholes(*pieces, *sources),
        out_specs=whole(size // cw, size),
        scratch_shapes=[pltpu.VMEM((size, width), BF)] * 2,
        compiler_params=PARAMS,
        name="column_sum",
    )(*held_in_hbm(*pieces, *sources))


def hidden_kernel(n, place, rows_in, x, own, *refs):
    received, (hidden, mixed) = refs[: n - 1], refs[n - 1 :]
    cw, lanes = own.shape
    side = pl.ds(pl.multiple_of(pl.program_id(0) * lanes, lanes), lanes)
    for i in range(n):
        spot = pl.multiple_of(lax.rem(place[0] + n - i, n) * cw, cw)
        mixed[pl.ds(spot, cw), :] = own[...] if i == 0 else received[i - 1][:, side]
    second = jnp.dot(rows_in[...], mixed[...], preferred_element_type=F)
    hidden[...] = (x[...].astype(F) + second).astype(BF)


def hidden_row(place, rows_in, inputs, h, pieces):
    cols, width = inputs.shape[1:]
    n = len(pieces)
    lanes = 512
    column = pl.BlockSpec((cols, lanes), lambda j: (0, j))
    return pl.pallas_call(
        functools.partial(hidden_kernel, n),
        out_shape=[shape_of((cols, width))] * 2,
        grid=(width // lanes,),
        in_specs=[
            SM,
            pl.BlockSpec((cols, cols), lambda j: (0, 0)),
            pl.BlockSpec((None, cols, lanes), lambda j: (h, 0, j)),
            pl.BlockSpec((cols // n, lanes), lambda j: (0, j)),
        ]
        + [VM] * (n - 1),
        out_specs=[column, column],
        name="hidden_row",
    )(place, *held_in_hbm(rows_in, inputs, pieces[0]), *pieces[1:])


def started(pairs, done):
    copies = [
        pltpu.make_async_copy(source, target, done.at[i])
        for i, (source, target) in enumerate(pairs)
    ]
    for copy in copies:
        copy.start()
    return copies


def channel_kernel(h, count, place, wg_own, wu_own, *refs):
    sources, results, held = refs[:count], refs[count : count + 6], refs[count + 6 : -3]
    mid, come, gone = refs[-3:]
    inputs, outs = held[:count], held[count:]
    views = [source.at[h] if len(source.shape) == len(buffer.shape) + 1 else source
             for source, buffer in zip(sources, inputs)]
    copies = started(list(zip(views, inputs)), come)
    h_own, h_oth, *lent = inputs[:6]
    mix_g, mix_u, c_own, c_oth, rows_in, mixed, *before = inputs[6:]
    hid_grad, back_g, back_u, turned, mix_sum, row_sum = outs
    mid_g, mid_u = mid.at[0], mid.at[1]
    local, size = wg_own.shape[:2]
    blocks = 2 * local
    cols = h_own.shape[0]
    copies[0].wait()
    for k in range(local):
        part = h_own[:, k * size : (k + 1) * size]
        mid_g[k] = jnp.dot(part, wg_own[k], preferred_element_type=F)
        mid_u[k] = jnp.dot(part, wu_own[k], preferred_element_type=F)
    core, x = place[2], place[3]
    copies[1].wait()
    for i, block in enumerate(lent):
        table = core if i < 2 else 1 - core
        k = x if i % 2 == 0 else 1 - x
        copies[2 + i].wait()
        part = h_oth[:, pl.ds(pl.multiple_of(k * size, size), size)]
        mid[table, local + k] = jnp.dot(part, block[...], preferred_element_type=F)
    for copy in copies[6:10]:
        copy.wait()
    mix_sum[...] = jnp.zeros_like(mix_sum)
    deep, lanes = 16, 128

    def chunk(t, carry):
        rows = pl.ds(pl.multiple_of(t * deep, deep), deep)
        for q in range(size // lanes):
            at = slice(q * lanes, (q + 1) * lanes)
            shape = (deep // 8, 8, lanes)
            g = [mid_g[k, rows, at].reshape(shape) for k in range(blocks)]
            u = [mid_u[k, rows, at].reshape(shape) for k in range(blocks)]
            sum_g, sum_u = [None] * local, [None] * local
            for m in range(blocks):
                c = c_own if m < local else c_oth
                start = (m % local) * size + q * lanes
                up = c[rows, start : start + lanes].astype(F).reshape(shape)
                gate_out = mix_g[m, 0, :, at] * g[0]
                up_out = mix_u[m, 0, :, at] * u[0]
                for k in range(1, blocks):
                    gate_out = gate_out + mix_g[m, k, :, at] * g[k]
                    up_out = up_out + mix_u[m, k, :, at] * u[k]
                sigma = 0.5 * jnp.tanh(0.5 * gate_out) + 0.5
                scaled = up * sigma
                up_grad = scaled * gate_out
                gate_grad = scaled * up_out * (1.0 + gate_out * (1.0 - sigma))
                for k in range(local):
                    mix_sum[0, m, k, :, at] += jnp.sum(gate_grad * g[k], axis=0)
                    mix_sum[1, m, k, :, at] += jnp.sum(up_grad * u[k], axis=0)
                    term_g = mix_g[m, k, :, at] * gate_grad
                    term_u = mix_u[m, k, :, at] * up_grad
                    sum_g[k] = term_g if m == 0 else sum_g[k] + term_g
                    sum_u[k] = term_u if m == 0 else sum_u[k] + term_u
            for k in range(local):
                spot = slice(k * size + q * lanes, k * size + (q + 1) * lanes)
                back_g[rows, spot] = sum_g[k].reshape(deep, lanes).astype(BF)
                back_u[rows, spot] = sum_u[k].reshape(deep, lanes).astype(BF)
        return carry

    lax.fori_loop(0, cols // deep, chunk, 0)
    leaving = [(outs[i], results[i]) for i in (1, 2, 4)]
    going = started(leaving, gone)
    for copy in copies[10:]:
        copy.wait()
    last = (((1,), (1,)), ((), ()))
    for k in range(local):
        spot = slice(k * size, (k + 1) * size)
        grad = lax.dot_general(back_g[:, spot], wg_own[k], last, preferred_element_type=F)
        grad = grad + lax.dot_general(back_u[:, spot], wu_own[k], last, preferred_element_type=F)
        hid_grad[:, spot] = (c_own[:, spot].astype(F) + grad).astype(BF)
    turned[...] = lax.dot_general(
        rows_in[...], hid_grad[...], (((0,), (0,)), ((), ())), preferred_element_type=F
    ).astype(BF)
    going += started([(outs[i], results[i]) for i in (0, 3)], gone.at[pl.ds(3, 2)])
    total = lax.dot_general(hid_grad[...], mixed[...], last, preferred_element_type=F)
    for value in before:
        total = value[...] + total
    row_sum[...] = total
    going += started([(outs[5], results[5])], gone.at[pl.ds(5, 1)])
    for copy in going:
        copy.wait()


def channel_row(place, h, h_own, h_oth, cot, cot_oth, weights, mixes, rows_in, mixed, before):
    cols, width = h_own.shape
    local, size = weights[0].shape[:2]
    blocks = 2 * local
    sources = (h_own, h_oth, *weights[2:], *mixes, cot, cot_oth, rows_in, mixed, *before)
    results = [((cols, width), BF)] * 4 + [((2, blocks, local, 8, size), F), ((cols, cols), F)]
    count = len(sources)
    buffers = [
        pltpu.VMEM(value.shape[1:] if value is cot or value is cot_oth else value.shape, value.dtype)
        for value in sources
    ]
    buffers += [pltpu.VMEM(*result) for result in results]
    return pl.pallas_call(
        functools.partial(channel_kernel, h, count),
        out_shape=[shape_of(*result) for result in results],
        in_specs=[SM] + [VM] * 2 + [pl.BlockSpec(memory_space=pltpu.HBM)] * count,
        out_specs=[pl.BlockSpec(memory_space=pltpu.HBM)] * 6,
        scratch_shapes=buffers
        + [
            pltpu.VMEM((2, blocks, cols, size), F),
            pltpu.SemaphoreType.DMA((count,)),
            pltpu.SemaphoreType.DMA((6,)),
        ],
        compiler_params=PARAMS,
        name="channel_row",
    )(place, *weights[:2], *held_in_hbm(*sources))


def sums_kernel(rows, parts, place, row_sum, *refs):
    hid, back_g, back_u, mix_sum = (refs[i * rows : (i + 1) * rows] for i in range(4))
    outs = refs[4 * rows :]
    size = outs[0].shape[-1]
    local = hid[0].shape[1] // size
    blocks = 2 * local
    first = (((0,), (0,)), ((), ()))
    high = local * size // parts
    per = size // high
    chan, core = place[1], place[2]
    for part, out in ((1, outs[1]), (0, outs[0])):
        k = core if part == 0 else 1 - core
        spot = pl.ds(pl.multiple_of(k * size, size), size)
        for w, back in enumerate((back_g, back_u)):
            total = None
            for h in range(rows):
                term = lax.dot_general(
                    hid[h][:, spot], back[h][:, spot], first, preferred_element_type=F
                )
                total = term if total is None else total + term
            for q in range(per):
                out[q, w * high : (w + 1) * high, :] = total[q * high : (q + 1) * high].astype(BF)
        for q in range(per):
            p = k * per + q
            m_at = lax.rem(p // (2 * local) + blocks - chan * local, blocks)
            k_at = lax.rem(p // 2, local)
            lines = [
                jnp.sum(sum(ref[w, m_at, k_at] for ref in mix_sum), axis=0, keepdims=True)
                for w in range(2)
            ]
            at = pl.multiple_of(p * 16, 16)
            eight = jnp.concatenate(
                [row_sum[pl.ds(at, 8), :], row_sum[pl.ds(at + 8, 8), :]], axis=1
            )
            tail = jnp.concatenate([eight, *lines, jnp.zeros((6, size), F)], axis=0)
            out[q, 2 * high :, :] = tail.astype(BF)


def sums(place, parts, row_sum, hid, back_g, back_u, mix_sum):
    rows = len(hid)
    size = mix_sum[0].shape[-1]
    high = hid[0].shape[1] // parts
    dims = (parts // 2, 2 * high + 16, size)
    return pl.pallas_call(
        once(functools.partial(sums_kernel, rows, parts)),
        out_shape=[shape_of(dims)] * 2,
        grid=(2,),
        in_specs=[SM] + wholes(row_sum, *hid, *back_g, *back_u, *mix_sum),
        out_specs=[whole(*dims)] * 2,
        compiler_params=PARAMS,
        name="sums",
    )(place, *held_in_hbm(row_sum, *hid, *back_g, *back_u, *mix_sum))


def core_add_kernel(n, place, kept, got, *outs):
    at, x = place[0], place[3]
    for i in range(n):
        for part in range(2):
            q = (x if part else 1 - x) * n + lax.rem(at + i, n)
            out = outs[n].at[i] if part else outs[i]
            out[...] = (kept[q].astype(F) + got[q].astype(F)).astype(BF)


def core_add(n, place, kept, got):
    deep, size = kept.shape[1:]
    return pl.pallas_call(
        once(functools.partial(core_add_kernel, n)),
        out_shape=[shape_of((deep, size))] * n + [shape_of((n, deep, size))],
        grid=(2,),
        in_specs=[SM] + wholes(kept, got),
        out_specs=[whole(deep, size)] * n + [whole(n, deep, size)],
        compiler_params=PARAMS,
        name="core_add",
    )(place, *held_in_hbm(kept), got)


def unpack_kernel(n, scales, place, *refs):
    held = refs[:4]
    gate, up, rows, mix_g, mix_u, cols_out, lines = refs[4:]
    local = mix_g.shape[1]
    at, core, x = place[0], place[2], place[3]
    high = gate.shape[0] // (4 * n)
    half = rows.shape[1]
    for i in range(4):
        base = lax.rem(core + i // 2, 2) * 2 * n + lax.rem(x + i % 2, 2) * n
        for j in range(n):
            p = base + lax.rem(at + n - j, n)
            spot = pl.ds(pl.multiple_of(p * high, high), high)
            gate[spot, :] = held[i][j, :high, :].astype(F) * scales[1]
            up[spot, :] = held[i][j, high : 2 * high, :].astype(F) * scales[1]
            tail = held[i][j, 2 * high :, :].astype(F)
            where = pl.multiple_of(p * 16, 16)
            rows[pl.ds(where, 8), :] = tail[:8, :half] * scales[0]
            rows[pl.ds(where + 8, 8), :] = tail[:8, half:] * scales[0]
            for w, out in enumerate((mix_g, mix_u)):
                spot = (pl.ds(p // (2 * local), 1), pl.ds(lax.rem(p // 2, local), 1), slice(None))
                out[spot] = tail[None, 8 + w : 9 + w, :] * scales[1]
            lines[pl.ds(p, 1), :] = tail[10:11, :] + tail[11:12, :]
    total = jnp.sum(lines[...], axis=0, keepdims=True) * scales[2]
    count = cols_out.shape[0]
    for r in range(count):
        cols_out[r : r + 1, :] = total[:, r * count : (r + 1) * count]


def unpack(n, rows, local, scales, place, held, cols):
    deep, size = held[0].shape[1:]
    high = (deep - 16) // 2
    return pl.pallas_call(
        functools.partial(unpack_kernel, n, scales),
        out_shape=[shape_of((4 * n * high, size), F)] * 2
        + [shape_of((cols, cols), F)]
        + [shape_of((2 * local, local, size), F)] * 2
        + [shape_of((n * rows, n * rows), F)],
        grid=(1,),
        in_specs=[SM] + wholes(*held),
        out_specs=[whole(4 * n * high, size)] * 2
        + [whole(cols, cols)]
        + [whole(2 * local, local, size)] * 2
        + [whole(n * rows, n * rows)],
        scratch_shapes=[pltpu.VMEM((4 * n, size), F)],
        compiler_params=PARAMS,
        name="unpack",
    )(place, *held)


def finish_kernel(grad, back, *refs):
    lanes = grad.shape[1]
    side = pl.ds(pl.multiple_of(pl.program_id(0) * lanes, lanes), lanes)
    refs[-1][...] = (grad[...].astype(F) + back[:, side].astype(F)).astype(BF)


def finish(h, rows, grad, back, before):
    cols, width = grad.shape
    lanes = 512
    return pl.pallas_call(
        finish_kernel,
        out_shape=shape_of((rows, cols, width)),
        grid=(width // lanes,),
        in_specs=[pl.BlockSpec((cols, lanes), lambda j: (0, j)), VM]
        + [pl.BlockSpec(memory_space=pltpu.HBM)] * len(before),
        out_specs=pl.BlockSpec((None, cols, lanes), lambda j: (h, 0, j)),
        input_output_aliases={2: 0} if before else {},
        name="finish",
    )(*held_in_hbm(grad), back, *before)


def shifted(value, by, n):
    return lax.ppermute(value, "seq", [(i, (i + by) % n) for i in range(n)])


def swapped(value, axis, bit, n):
    return lax.ppermute(value, axis, [(i, i ^ bit) for i in range(n)])


def traded(value):
    return lax.all_to_all(value, "seq", split_axis=0, concat_axis=0, tiled=True)


def pick(value, index):
    return lax.dynamic_index_in_dim(value, index, 0, keepdims=False)


def add(*values):
    return sum(value.astype(F) for value in values).astype(BF)


def two_lines(line):
    upper = line.astype(BF)
    return upper, (line - upper.astype(F)).astype(BF)


def two_lines(line):
    upper = line.astype(BF)
    return upper, (line - upper.astype(F)).astype(BF)


def scatter_seq(by_x, fours, cols_sum, n):
    deep, size = fours.shape[1:]
    arrived = []
    for i in [*range(1, n), 0]:
        shard = add(fours[i], by_x[i])
        arrived.append(shifted(shard, i, n) if i else shard)
    count = cols_sum.size
    line = jnp.pad(cols_sum.reshape(1, count), ((0, 0), (0, size - count)))
    lines = jnp.pad(jnp.concatenate(two_lines(line), axis=0), ((deep - 6, 4), (0, 0)))
    mine = add(*arrived, lines)
    tail = mine[deep - 16 :]
    other = swapped(tail, "chan", 1, 2)
    both = tail.astype(F) + other.astype(F)
    lines = two_lines(both[10:11] + both[11:12])
    tail = jnp.concatenate([both[:8].astype(BF), tail[8:10], *lines, tail[12:]], axis=0)
    return jnp.concatenate([mine[: deep - 16], tail], axis=0)


def block_body(inputs, cotangent, rows_in, cols_mix, blocks_gate, blocks_up, mix_gate, mix_up):
    n = lax.axis_size("seq")
    rows, cols, width = inputs.shape[1:]
    local, size = blocks_gate.shape[:2]
    cw = cols // n
    seq_at, chan_at, dp_at = lax.axis_index("seq"), lax.axis_index("chan"), lax.axis_index("dp")
    core, x = lax.rem(dp_at, 2), dp_at // 2
    place = jnp.stack([seq_at, chan_at, core, x]).astype(jnp.int32)
    values, cot = inputs[0], cotangent[0]
    ahead, behind = mix_tables(cols_mix, seq_at, n, rows, cw)

    def relative(table):
        turned = jnp.roll(table, (local, local), (0, 1))
        table = jnp.where(chan_at == 0, table, turned).astype(F)
        return jnp.broadcast_to(table[:, :, None, :], table.shape[:2] + (8, size))

    ways = [
        lax.dynamic_slice_in_dim(values, lax.rem(seq_at + i, n) * cw, cw, 1) for i in range(n)
    ]
    x_cols = [ways[0]] + [shifted(ways[i], i, n) for i in range(1, n)]
    x_cols = [part.reshape(rows * cw, width) for part in x_cols]
    lent = pick(jnp.where(core == 0, blocks_gate, blocks_up), x)
    lent = swapped(lent, "chan", 1, 2)
    leaving, _ = lax.optimization_barrier((cot, lent))
    cot_oth = swapped(leaving, "chan", 1, 2)
    lent = [lent, swapped(lent, "dp", 2, 4)]
    mixes = (relative(mix_gate), relative(mix_up))

    x_cols, ahead, behind, mixes = lax.optimization_barrier((x_cols, ahead, behind, mixes))
    parts = column_mix(ahead, x_cols, n * rows, "column_mix")
    parts, lent = lax.optimization_barrier((parts, lent))
    passed = [swapped(block, "dp", 1, 4) for block in lent]
    parts = list(parts)
    held_up = [i for i in range(n * rows) if i not in (0, rows, 2 * rows)]
    late, passed = lax.optimization_barrier(([parts[i] for i in held_up], passed))
    for i, part in zip(held_up, late):
        parts[i] = part
    lent = lent + passed
    got = [
        [parts[h]] + [shifted(parts[i * rows + h], i, n) for i in range(1, n)]
        for h in range(rows)
    ]
    got[0], cot_oth = lax.optimization_barrier((got[0], cot_oth))
    hidden, mixed = [], []
    for h in range(rows):
        for held, value in zip((hidden, mixed), hidden_row(place, rows_in, values, h, got[h])):
            held.append(value)
    weights = (blocks_gate, blocks_up, *lent)
    others = [swapped(hid, "chan", 1, 2) for hid in hidden]
    others[0], hidden[-1] = lax.optimization_barrier((others[0], hidden[-1]))
    grads, back_g, back_u, pieces, mix_sum, rows_sum = [], [], [], [], [], []
    for h in range(rows):
        got = channel_row(
            place,
            h,
            hidden[h],
            others[h],
            cot,
            cot_oth,
            weights,
            mixes,
            rows_in,
            mixed[h],
            rows_sum,
        )
        for held, value in zip((grads, back_g, back_u, pieces, mix_sum), got):
            held.append(value)
        rows_sum = got[5:]
    kept, sent = sums(place, 4 * n, rows_sum[0], hidden, back_g, back_u, mix_sum)
    pieces[0], _ = lax.optimization_barrier((pieces[0], others[-1]))
    pieces[0] = traded(pieces[0].reshape(n, cw, width)).reshape(cols, width)
    sent, _ = lax.optimization_barrier((sent, pieces[0]))
    pieces[1], _ = lax.optimization_barrier((pieces[1], kept))
    pieces[1] = traded(pieces[1].reshape(n, cw, width)).reshape(cols, width)
    *leaving, fours = core_add(n, place, kept, swapped(sent, "dp", 1, 4))
    by_x = [swapped(shard, "dp", 2, 4) for shard in leaving]
    pieces[1], _ = lax.optimization_barrier((pieces[1], by_x[1]))
    turned = column_mix(behind, pieces, rows, "column_back")
    backs = [traded(turned[0].reshape(n, cw, width))]
    late, _ = lax.optimization_barrier((pieces[1], turned[0]))
    cols_sum = column_sum(cw, x_cols, [pieces[0], late])
    cols_sum = cols_sum.reshape(rows, n, n * rows, cw).sum(-1).transpose(1, 0, 2)
    cols_sum = turned_blocks(cols_sum.reshape(n * rows, n * rows), seq_at, -1, n, rows, 1)
    mine = scatter_seq(by_x, fours, cols_sum, n)
    held = [mine] + [shifted(mine, i, n) for i in range(1, n)]
    for part in turned[1:]:
        part, _ = lax.optimization_barrier((part, held[1]))
        backs.append(traded(part.reshape(n, cw, width)))
    backs = [part.reshape(cols, width) for part in backs]
    batch_all = lax.axis_size("dp")
    width_all = width * lax.axis_size("chan")
    rows_scale = 1.0 / math.sqrt(batch_all * rows * n * width_all)
    cols_scale = 1.0 / math.sqrt(batch_all * cols * width_all)
    block_scale = 1.0 / math.sqrt(batch_all * rows * n * cols)
    by_x = jnp.stack([swapped(shard, "dp", 2, 4) for shard in held])
    held = jnp.stack(held)
    by_core = swapped(held, "dp", 1, 4)
    done = []
    for h in range(rows):
        done = [finish(h, rows, grads[h], backs[h], done)]
    input_grad = done[0]
    gate_sum, up_sum, rows_sum, mix_g, mix_u, cols_sum = unpack(
        n,
        rows,
        local,
        (rows_scale, block_scale, cols_scale),
        place,
        (held, by_x, by_core, swapped(by_x, "dp", 1, 4)),
        cols,
    )
    return (
        input_grad[None],
        rows_sum,
        cols_sum,
        gate_sum.reshape(local, size, size),
        up_sum.reshape(local, size, size),
        mix_g,
        mix_u,
    )


def column_keep(segment, cols_mix):
    mixed = jnp.einsum(
        "er,brcd->becd", cols_mix, segment, preferred_element_type=jnp.float32
    ).astype(jnp.bfloat16)
    return (segment, mixed)

def body(inputs, cotangent, rows_in, cols_mix, blocks_gate, blocks_up, mix_gate, mix_up):
    batch_dev, rows_dev, cols_all, width_dev = inputs.shape
    block_size = blocks_gate.shape[1]
    local_blocks = blocks_gate.shape[0]
    chan_index = lax.axis_index("chan")
    split_shape = (batch_dev, rows_dev, cols_all, local_blocks, block_size)
    first = jnp.einsum("ec,brcd->bred", rows_in, inputs, preferred_element_type=jnp.float32).astype(
        jnp.bfloat16
    )
    first_cols, second_cols = column_keep(
        lax.all_to_all(first, "seq", split_axis=2, concat_axis=1, tiled=True), cols_mix
    )
    second_rows = lax.all_to_all(second_cols, "seq", split_axis=1, concat_axis=2, tiled=True)
    hidden = (inputs.astype(jnp.float32) + second_rows.astype(jnp.float32)).astype(jnp.bfloat16)
    hidden_blocks = hidden.reshape(split_shape)
    gate_rows_own = lax.dynamic_slice_in_dim(
        mix_gate, chan_index * local_blocks, local_blocks, 0
    ).astype(jnp.float32)
    up_rows_own = lax.dynamic_slice_in_dim(
        mix_up, chan_index * local_blocks, local_blocks, 0
    ).astype(jnp.float32)
    gate_mid = jnp.einsum(
        "brckj,kjl->brckl", hidden_blocks, blocks_gate, preferred_element_type=jnp.float32
    ).astype(jnp.bfloat16)
    up_mid = jnp.einsum(
        "brckj,kjl->brckl", hidden_blocks, blocks_up, preferred_element_type=jnp.float32
    ).astype(jnp.bfloat16)
    gate_add = jnp.einsum(
        "mkj,brckj->brcmj",
        gate_rows_own,
        lax.all_gather(gate_mid, "chan", axis=3, tiled=True).astype(jnp.float32),
    )
    up_add = jnp.einsum(
        "mkj,brckj->brcmj",
        up_rows_own,
        lax.all_gather(up_mid, "chan", axis=3, tiled=True).astype(jnp.float32),
    )
    upstream = cotangent.astype(jnp.float32).reshape(split_shape)
    sigma = jax.nn.sigmoid(gate_add)
    up_grad = (upstream * gate_add * sigma).astype(jnp.bfloat16)
    gate_grad = (upstream * up_add * sigma * (1.0 + gate_add * (1.0 - sigma))).astype(jnp.bfloat16)
    gate_all, up_all = (
        lax.all_gather(gate_grad, "chan", axis=3, tiled=True),
        lax.all_gather(up_grad, "chan", axis=3, tiled=True),
    )
    gate_cols_own = lax.dynamic_slice_in_dim(
        mix_gate, chan_index * local_blocks, local_blocks, 1
    ).astype(jnp.float32)
    up_cols_own = lax.dynamic_slice_in_dim(
        mix_up, chan_index * local_blocks, local_blocks, 1
    ).astype(jnp.float32)
    mix_gate_sum = jnp.einsum(
        "brcmj,brckj->mkj", gate_all, gate_mid, preferred_element_type=jnp.float32
    )
    mix_up_sum = jnp.einsum("brcmj,brckj->mkj", up_all, up_mid, preferred_element_type=jnp.float32)
    gate_back = jnp.einsum("mkj,brcmj->brckj", gate_cols_own, gate_all.astype(jnp.float32)).astype(
        jnp.bfloat16
    )
    up_back = jnp.einsum("mkj,brcmj->brckj", up_cols_own, up_all.astype(jnp.float32)).astype(
        jnp.bfloat16
    )
    blocks_gate_sum = jnp.einsum(
        "brckj,brckl->kjl", hidden_blocks, gate_back, preferred_element_type=jnp.float32
    )
    blocks_up_sum = jnp.einsum(
        "brckj,brckl->kjl", hidden_blocks, up_back, preferred_element_type=jnp.float32
    )
    hidden_grad = (
        upstream
        + jnp.einsum("brckl,kjl->brckj", gate_back, blocks_gate, preferred_element_type=jnp.float32)
        + jnp.einsum("brckl,kjl->brckj", up_back, blocks_up, preferred_element_type=jnp.float32)
    )
    hidden_grad = hidden_grad.reshape(inputs.shape).astype(jnp.bfloat16)
    segment = lax.all_to_all(hidden_grad, "seq", split_axis=2, concat_axis=1, tiled=True)
    mixed = jnp.einsum(
        "er,becd->brcd", cols_mix, segment, preferred_element_type=jnp.float32
    ).astype(jnp.bfloat16)
    cols_sum = jnp.einsum("becd,brcd->er", segment, first_cols, preferred_element_type=jnp.float32)
    first_grad = lax.all_to_all(mixed, "seq", split_axis=1, concat_axis=2, tiled=True)
    rows_sum = jnp.einsum("bred,brcd->ec", first_grad, inputs, preferred_element_type=jnp.float32)
    input_grad = (
        hidden_grad.astype(jnp.float32)
        + jnp.einsum("ec,bred->brcd", rows_in, first_grad, preferred_element_type=jnp.float32)
    ).astype(jnp.bfloat16)
    rows_total, cols_total = lax.psum((rows_sum, cols_sum), ("dp", "seq", "chan"))
    gate_blocks_total, up_blocks_total, gate_mix_total, up_mix_total = lax.psum(
        (blocks_gate_sum, blocks_up_sum, mix_gate_sum, mix_up_sum), ("dp", "seq")
    )
    count_dp = lax.axis_size("dp")
    count_seq = lax.axis_size("seq")
    count_chan = lax.axis_size("chan")
    batch_all = batch_dev * count_dp
    rows_all = rows_dev * count_seq
    width_all = width_dev * count_chan
    rows_scale = 1.0 / math.sqrt(batch_all * rows_all * width_all)
    cols_scale = 1.0 / math.sqrt(batch_all * cols_all * width_all)
    block_scale = 1.0 / math.sqrt(batch_all * rows_all * cols_all)
    return (
        input_grad,
        rows_total * rows_scale,
        cols_total * cols_scale,
        gate_blocks_total * block_scale,
        up_blocks_total * block_scale,
        gate_mix_total * block_scale,
        up_mix_total * block_scale,
    )


def solution(mesh):
    in_specs = (
        P("dp", "seq", None, "chan"),
        P("dp", "seq", None, "chan"),
        P(),
        P(),
        P("chan", None, None),
        P("chan", None, None),
        P(),
        P(),
    )
    out_specs = (
        P("dp", "seq", None, "chan"),
        P(),
        P(),
        P("chan", None, None),
        P("chan", None, None),
        P(None, "chan", None),
        P(None, "chan", None),
    )
    sizes = dict(mesh.shape)
    fits = sizes["dp"] == 4 and sizes["seq"] == 4 and sizes["chan"] == 2
    return jax.shard_map(block_body if fits else body, mesh=mesh, in_specs=in_specs, out_specs=out_specs, check_vma=False)
```

```python
import functools
import math

import jax
import jax.numpy as jnp
from jax import lax
from jax.experimental import pallas as pl
from jax.experimental.pallas import tpu as pltpu
from jax.sharding import PartitionSpec as P

BF = jnp.bfloat16
F = jnp.float32
VM = pl.BlockSpec(memory_space=pltpu.VMEM)
SM = pl.BlockSpec(memory_space=pltpu.SMEM)
PARAMS = pltpu.CompilerParams(vmem_limit_bytes=20 * 1024 * 1024)


def whole(*dims):
    return pl.BlockSpec(dims, lambda j: (0,) * len(dims))


def wholes(*values):
    return [whole(*value.shape) for value in values]


def once(kernel):
    def run(*refs):
        @pl.when(pl.program_id(0) == 0)
        def _():
            kernel(*refs)

    return run


def held_in_hbm(*values):
    return [pltpu.with_memory_space_constraint(value, pltpu.HBM) for value in values]


def shape_of(dims, kind=BF):
    return pltpu.HBM(dims, kind)


def turned_blocks(table, at, step, n, rows, axis):
    return jnp.concatenate(
        [
            lax.dynamic_slice_in_dim(table, lax.rem(at + n + step * j, n) * rows, rows, axis)
            for j in range(n)
        ],
        axis=axis,
    )


def mix_tables(mix, at, n, rows, cw):
    size = mix.shape[0]
    same = lax.broadcasted_iota(jnp.int32, (1, cw, 1, cw), 1) == lax.broadcasted_iota(
        jnp.int32, (1, cw, 1, cw), 3
    )

    def spread(table):
        grown = jnp.where(same, table[:, None, :, None], jnp.zeros((), BF))
        return grown.reshape(size * cw, size * cw)

    ahead = turned_blocks(turned_blocks(mix, at, -1, n, rows, 1), at, 1, n, rows, 0)
    back = mix.T.reshape(n, rows, n, rows).transpose(1, 0, 3, 2).reshape(size, size)
    return spread(ahead), spread(back)


def column_mix_kernel(count, table, *refs):
    sources, outs = refs[:count], refs[count:]
    whole_source = jnp.concatenate([source[...] for source in sources], axis=0)
    total = jnp.dot(table[...], whole_source, preferred_element_type=F).astype(BF)
    deep = outs[0].shape[0]
    for i, out in enumerate(outs):
        out[...] = total[i * deep : (i + 1) * deep]


def column_mix(table, sources, outs, name):
    size = table.shape[0]
    width = sources[0].shape[-1]
    lanes = 512
    deep = size // outs
    return pl.pallas_call(
        functools.partial(column_mix_kernel, len(sources)),
        out_shape=[shape_of((deep, width))] * outs,
        grid=(width // lanes,),
        in_specs=[pl.BlockSpec((size, size), lambda j: (0, 0))]
        + [pl.BlockSpec((source.shape[0], lanes), lambda j: (0, j)) for source in sources],
        out_specs=[pl.BlockSpec((deep, lanes), lambda j: (0, j))] * outs,
        name=name,
    )(*held_in_hbm(table), *sources)


def column_sum_kernel(cw, rows, *refs):
    pieces, sources, (out, left, right) = refs[:rows], refs[rows:-3], refs[-3:]
    for side, parts in ((left, pieces), (right, sources)):
        deep = parts[0].shape[0]
        for j, part in enumerate(parts):
            side[j * deep : (j + 1) * deep, :] = part[...]
    product = lax.dot_general(
        left[...], right[...], (((1,), (1,)), ((), ())), preferred_element_type=F
    )
    size = product.shape[0]
    row_at = lax.broadcasted_iota(jnp.int32, (size, size), 0)
    col_at = lax.broadcasted_iota(jnp.int32, (size, size), 1)
    kept = jnp.where(lax.rem(row_at, cw) == lax.rem(col_at, cw), product, 0.0)
    out[...] = jnp.sum(kept.reshape(size // cw, cw, size), axis=1)


def column_sum(cw, sources, pieces):
    width = pieces[0].shape[1]
    size = sum(piece.shape[0] for piece in pieces)
    return pl.pallas_call(
        once(functools.partial(column_sum_kernel, cw, len(pieces))),
        out_shape=shape_of((size // cw, size), F),
        grid=(2,),
        in_specs=wholes(*pieces, *sources),
        out_specs=whole(size // cw, size),
        scratch_shapes=[pltpu.VMEM((size, width), BF)] * 2,
        compiler_params=PARAMS,
        name="column_sum",
    )(*held_in_hbm(*pieces, *sources))


def hidden_kernel(n, place, rows_in, x, own, *refs):
    received, (hidden, mixed) = refs[: n - 1], refs[n - 1 :]
    cw, lanes = own.shape
    side = pl.ds(pl.multiple_of(pl.program_id(0) * lanes, lanes), lanes)
    for i in range(n):
        spot = pl.multiple_of(lax.rem(place[0] + n - i, n) * cw, cw)
        mixed[pl.ds(spot, cw), :] = own[...] if i == 0 else received[i - 1][:, side]
    second = jnp.dot(rows_in[...], mixed[...], preferred_element_type=F)
    hidden[...] = (x[...].astype(F) + second).astype(BF)


def hidden_row(place, rows_in, inputs, h, pieces):
    cols, width = inputs.shape[1:]
    n = len(pieces)
    lanes = 512
    column = pl.BlockSpec((cols, lanes), lambda j: (0, j))
    return pl.pallas_call(
        functools.partial(hidden_kernel, n),
        out_shape=[shape_of((cols, width))] * 2,
        grid=(width // lanes,),
        in_specs=[
            SM,
            pl.BlockSpec((cols, cols), lambda j: (0, 0)),
            pl.BlockSpec((None, cols, lanes), lambda j: (h, 0, j)),
            pl.BlockSpec((cols // n, lanes), lambda j: (0, j)),
        ]
        + [VM] * (n - 1),
        out_specs=[column, column],
        name="hidden_row",
    )(place, *held_in_hbm(rows_in, inputs, pieces[0]), *pieces[1:])


def started(pairs, done):
    copies = [
        pltpu.make_async_copy(source, target, done.at[i])
        for i, (source, target) in enumerate(pairs)
    ]
    for copy in copies:
        copy.start()
    return copies


def channel_kernel(h, count, place, wg_own, wu_own, *refs):
    sources, results, held = refs[:count], refs[count : count + 6], refs[count + 6 : -3]
    mid, come, gone = refs[-3:]
    inputs, outs = held[:count], held[count:]
    views = [source.at[h] if len(source.shape) == len(buffer.shape) + 1 else source
             for source, buffer in zip(sources, inputs)]
    copies = started(list(zip(views, inputs)), come)
    h_own, h_oth, *lent = inputs[:6]
    mix_g, mix_u, c_own, c_oth, rows_in, mixed, *before = inputs[6:]
    hid_grad, back_g, back_u, turned, mix_sum, row_sum = outs
    mid_g, mid_u = mid.at[0], mid.at[1]
    local, size = wg_own.shape[:2]
    blocks = 2 * local
    cols = h_own.shape[0]
    copies[0].wait()
    for k in range(local):
        part = h_own[:, k * size : (k + 1) * size]
        mid_g[k] = jnp.dot(part, wg_own[k], preferred_element_type=F)
        mid_u[k] = jnp.dot(part, wu_own[k], preferred_element_type=F)
    core, x = place[2], place[3]
    copies[1].wait()
    for i, block in enumerate(lent):
        table = core if i < 2 else 1 - core
        k = x if i % 2 == 0 else 1 - x
        copies[2 + i].wait()
        part = h_oth[:, pl.ds(pl.multiple_of(k * size, size), size)]
        mid[table, local + k] = jnp.dot(part, block[...], preferred_element_type=F)
    for copy in copies[6:10]:
        copy.wait()
    mix_sum[...] = jnp.zeros_like(mix_sum)
    deep, lanes = 16, 128

    def chunk(t, carry):
        rows = pl.ds(pl.multiple_of(t * deep, deep), deep)
        for q in range(size // lanes):
            at = slice(q * lanes, (q + 1) * lanes)
            shape = (deep // 8, 8, lanes)
            g = [mid_g[k, rows, at].reshape(shape) for k in range(blocks)]
            u = [mid_u[k, rows, at].reshape(shape) for k in range(blocks)]
            sum_g, sum_u = [None] * local, [None] * local
            for m in range(blocks):
                c = c_own if m < local else c_oth
                start = (m % local) * size + q * lanes
                up = c[rows, start : start + lanes].astype(F).reshape(shape)
                gate_out = mix_g[m, 0, :, at] * g[0]
                up_out = mix_u[m, 0, :, at] * u[0]
                for k in range(1, blocks):
                    gate_out = gate_out + mix_g[m, k, :, at] * g[k]
                    up_out = up_out + mix_u[m, k, :, at] * u[k]
                sigma = 0.5 * jnp.tanh(0.5 * gate_out) + 0.5
                scaled = up * sigma
                up_grad = scaled * gate_out
                gate_grad = scaled * up_out * (1.0 + gate_out * (1.0 - sigma))
                for k in range(local):
                    mix_sum[0, m, k, :, at] += jnp.sum(gate_grad * g[k], axis=0)
                    mix_sum[1, m, k, :, at] += jnp.sum(up_grad * u[k], axis=0)
                    term_g = mix_g[m, k, :, at] * gate_grad
                    term_u = mix_u[m, k, :, at] * up_grad
                    sum_g[k] = term_g if m == 0 else sum_g[k] + term_g
                    sum_u[k] = term_u if m == 0 else sum_u[k] + term_u
            for k in range(local):
                spot = slice(k * size + q * lanes, k * size + (q + 1) * lanes)
                back_g[rows, spot] = sum_g[k].reshape(deep, lanes).astype(BF)
                back_u[rows, spot] = sum_u[k].reshape(deep, lanes).astype(BF)
        return carry

    lax.fori_loop(0, cols // deep, chunk, 0)
    leaving = [(outs[i], results[i]) for i in (1, 2, 4)]
    going = started(leaving, gone)
    for copy in copies[10:]:
        copy.wait()
    last = (((1,), (1,)), ((), ()))
    for k in range(local):
        spot = slice(k * size, (k + 1) * size)
        grad = lax.dot_general(back_g[:, spot], wg_own[k], last, preferred_element_type=F)
        grad = grad + lax.dot_general(back_u[:, spot], wu_own[k], last, preferred_element_type=F)
        hid_grad[:, spot] = (c_own[:, spot].astype(F) + grad).astype(BF)
    turned[...] = lax.dot_general(
        rows_in[...], hid_grad[...], (((0,), (0,)), ((), ())), preferred_element_type=F
    ).astype(BF)
    going += started([(outs[i], results[i]) for i in (0, 3)], gone.at[pl.ds(3, 2)])
    total = lax.dot_general(hid_grad[...], mixed[...], last, preferred_element_type=F)
    for value in before:
        total = value[...] + total
    row_sum[...] = total
    going += started([(outs[5], results[5])], gone.at[pl.ds(5, 1)])
    for copy in going:
        copy.wait()


def channel_row(place, h, h_own, h_oth, cot, cot_oth, weights, mixes, rows_in, mixed, before):
    cols, width = h_own.shape
    local, size = weights[0].shape[:2]
    blocks = 2 * local
    sources = (h_own, h_oth, *weights[2:], *mixes, cot, cot_oth, rows_in, mixed, *before)
    results = [((cols, width), BF)] * 4 + [((2, blocks, local, 8, size), F), ((cols, cols), F)]
    count = len(sources)
    buffers = [
        pltpu.VMEM(value.shape[1:] if value is cot or value is cot_oth else value.shape, value.dtype)
        for value in sources
    ]
    buffers += [pltpu.VMEM(*result) for result in results]
    return pl.pallas_call(
        functools.partial(channel_kernel, h, count),
        out_shape=[shape_of(*result) for result in results],
        in_specs=[SM] + [VM] * 2 + [pl.BlockSpec(memory_space=pltpu.HBM)] * count,
        out_specs=[pl.BlockSpec(memory_space=pltpu.HBM)] * 6,
        scratch_shapes=buffers
        + [
            pltpu.VMEM((2, blocks, cols, size), F),
            pltpu.SemaphoreType.DMA((count,)),
            pltpu.SemaphoreType.DMA((6,)),
        ],
        compiler_params=PARAMS,
        name="channel_row",
    )(place, *weights[:2], *held_in_hbm(*sources))


def sums_kernel(rows, parts, place, row_sum, *refs):
    hid, back_g, back_u, mix_sum = (refs[i * rows : (i + 1) * rows] for i in range(4))
    kept, sent, ready, done = refs[4 * rows :]
    cols, size = hid[0].shape
    blocks, local = mix_sum[0].shape[1:3]
    first = (((0,), (0,)), ((), ()))
    high = local * size // parts
    per = size // high
    chan, core = place[1], place[2]

    def half(k, out):
        for w, back in enumerate((back_g, back_u)):
            total = None
            for h in range(rows):
                term = lax.dot_general(
                    hid[h][...], back[h][...], first, preferred_element_type=F
                )
                total = term if total is None else total + term
            for q in range(per):
                out[q, w * high : (w + 1) * high, :] = total[q * high : (q + 1) * high].astype(BF)
        for q in range(per):
            p = k * per + q
            m_at = lax.rem(p // (2 * local) + blocks - chan * local, blocks)
            k_at = lax.rem(p // 2, local)
            lines = [
                jnp.sum(sum(ref[w, m_at, k_at] for ref in mix_sum), axis=0, keepdims=True)
                for w in range(2)
            ]
            at = pl.multiple_of(p * 16, 16)
            eight = jnp.concatenate(
                [row_sum[pl.ds(at, 8), :], row_sum[pl.ds(at + 8, 8), :]], axis=1
            )
            tail = jnp.concatenate([eight, *lines, jnp.zeros((6, size), F)], axis=0)
            out[q, 2 * high :, :] = tail.astype(BF)

    copy = pltpu.make_async_copy(ready, sent, done.at[0])

    @pl.when(pl.program_id(0) == 0)
    def _():
        half(1 - core, ready)
        copy.start()

    @pl.when(pl.program_id(0) == 1)
    def _():
        half(core, kept)
        copy.wait()


def sums(place, parts, row_sum, hid, back_g, back_u, mix_sum):
    rows = len(hid)
    cols, width = hid[0].shape
    size = mix_sum[0].shape[-1]
    high = width // parts
    dims = (parts // 2, 2 * high + 16, size)
    fixed = lambda *shape: pl.BlockSpec(shape, lambda j, at: (0,) * len(shape))
    side = pl.BlockSpec((cols, size), lambda j, at: (0, at[2] + (1 - j) * (1 - 2 * at[2])))
    return pl.pallas_call(
        functools.partial(sums_kernel, rows, parts),
        out_shape=[shape_of(dims)] * 2,
        grid_spec=pltpu.PrefetchScalarGridSpec(
            num_scalar_prefetch=1,
            grid=(2,),
            in_specs=[fixed(*row_sum.shape)]
            + [side] * (3 * rows)
            + [fixed(*value.shape) for value in mix_sum],
            out_specs=[fixed(*dims), pl.BlockSpec(memory_space=pltpu.HBM)],
            scratch_shapes=[pltpu.VMEM(dims, BF), pltpu.SemaphoreType.DMA((1,))],
        ),
        compiler_params=PARAMS,
        name="sums",
    )(place, *held_in_hbm(row_sum, *hid, *back_g, *back_u, *mix_sum))


def core_add_kernel(n, place, kept, got, *outs):
    at, x = place[0], place[3]
    for i in range(n):
        for part in range(2):
            q = (x if part else 1 - x) * n + lax.rem(at + i, n)
            out = outs[n].at[i] if part else outs[i]
            out[...] = (kept[q].astype(F) + got[q].astype(F)).astype(BF)


def core_add(n, place, kept, got):
    deep, size = kept.shape[1:]
    return pl.pallas_call(
        once(functools.partial(core_add_kernel, n)),
        out_shape=[shape_of((deep, size))] * n + [shape_of((n, deep, size))],
        grid=(2,),
        in_specs=[SM] + wholes(kept, got),
        out_specs=[whole(deep, size)] * n + [whole(n, deep, size)],
        compiler_params=PARAMS,
        name="core_add",
    )(place, *held_in_hbm(kept), got)


def unpack_kernel(n, scales, place, *refs):
    held = refs[:4]
    gate, up, rows, mix_g, mix_u, cols_out, lines = refs[4:]
    local = mix_g.shape[1]
    at, core, x = place[0], place[2], place[3]
    high = gate.shape[0] // (4 * n)
    half = rows.shape[1]
    for i in range(4):
        base = lax.rem(core + i // 2, 2) * 2 * n + lax.rem(x + i % 2, 2) * n
        for j in range(n):
            p = base + lax.rem(at + n - j, n)
            spot = pl.ds(pl.multiple_of(p * high, high), high)
            gate[spot, :] = held[i][j, :high, :].astype(F) * scales[1]
            up[spot, :] = held[i][j, high : 2 * high, :].astype(F) * scales[1]
            tail = held[i][j, 2 * high :, :].astype(F)
            where = pl.multiple_of(p * 16, 16)
            rows[pl.ds(where, 8), :] = tail[:8, :half] * scales[0]
            rows[pl.ds(where + 8, 8), :] = tail[:8, half:] * scales[0]
            for w, out in enumerate((mix_g, mix_u)):
                spot = (pl.ds(p // (2 * local), 1), pl.ds(lax.rem(p // 2, local), 1), slice(None))
                out[spot] = tail[None, 8 + w : 9 + w, :] * scales[1]
            lines[pl.ds(p, 1), :] = tail[10:11, :] + tail[11:12, :]
    total = jnp.sum(lines[...], axis=0, keepdims=True) * scales[2]
    count = cols_out.shape[0]
    for r in range(count):
        cols_out[r : r + 1, :] = total[:, r * count : (r + 1) * count]


def unpack(n, rows, local, scales, place, held, cols):
    deep, size = held[0].shape[1:]
    high = (deep - 16) // 2
    return pl.pallas_call(
        functools.partial(unpack_kernel, n, scales),
        out_shape=[shape_of((4 * n * high, size), F)] * 2
        + [shape_of((cols, cols), F)]
        + [shape_of((2 * local, local, size), F)] * 2
        + [shape_of((n * rows, n * rows), F)],
        grid=(1,),
        in_specs=[SM] + wholes(*held),
        out_specs=[whole(4 * n * high, size)] * 2
        + [whole(cols, cols)]
        + [whole(2 * local, local, size)] * 2
        + [whole(n * rows, n * rows)],
        scratch_shapes=[pltpu.VMEM((4 * n, size), F)],
        compiler_params=PARAMS,
        name="unpack",
    )(place, *held)


def finish_kernel(grad, back, *refs):
    lanes = grad.shape[1]
    side = pl.ds(pl.multiple_of(pl.program_id(0) * lanes, lanes), lanes)
    refs[-1][...] = (grad[...].astype(F) + back[:, side].astype(F)).astype(BF)


def finish(h, rows, grad, back, before):
    cols, width = grad.shape
    lanes = 512
    return pl.pallas_call(
        finish_kernel,
        out_shape=shape_of((rows, cols, width)),
        grid=(width // lanes,),
        in_specs=[pl.BlockSpec((cols, lanes), lambda j: (0, j)), VM]
        + [pl.BlockSpec(memory_space=pltpu.HBM)] * len(before),
        out_specs=pl.BlockSpec((None, cols, lanes), lambda j: (h, 0, j)),
        input_output_aliases={2: 0} if before else {},
        name="finish",
    )(*held_in_hbm(grad), back, *before)


def shifted(value, by, n):
    return lax.ppermute(value, "seq", [(i, (i + by) % n) for i in range(n)])


def swapped(value, axis, bit, n):
    return lax.ppermute(value, axis, [(i, i ^ bit) for i in range(n)])


def traded(value):
    return lax.all_to_all(value, "seq", split_axis=0, concat_axis=0, tiled=True)


def pick(value, index):
    return lax.dynamic_index_in_dim(value, index, 0, keepdims=False)


def add(*values):
    return sum(value.astype(F) for value in values).astype(BF)


def two_lines(line):
    upper = line.astype(BF)
    return upper, (line - upper.astype(F)).astype(BF)


def two_lines(line):
    upper = line.astype(BF)
    return upper, (line - upper.astype(F)).astype(BF)


def scatter_seq(by_x, fours, cols_sum, n):
    deep, size = fours.shape[1:]
    arrived = []
    for i in [*range(1, n), 0]:
        shard = add(fours[i], by_x[i])
        arrived.append(shifted(shard, i, n) if i else shard)
    count = cols_sum.size
    line = jnp.pad(cols_sum.reshape(1, count), ((0, 0), (0, size - count)))
    lines = jnp.pad(jnp.concatenate(two_lines(line), axis=0), ((deep - 6, 4), (0, 0)))
    mine = add(*arrived, lines)
    tail = mine[deep - 16 :]
    other = swapped(tail, "chan", 1, 2)
    both = tail.astype(F) + other.astype(F)
    lines = two_lines(both[10:11] + both[11:12])
    tail = jnp.concatenate([both[:8].astype(BF), tail[8:10], *lines, tail[12:]], axis=0)
    return jnp.concatenate([mine[: deep - 16], tail], axis=0)


def block_body(inputs, cotangent, rows_in, cols_mix, blocks_gate, blocks_up, mix_gate, mix_up):
    n = lax.axis_size("seq")
    rows, cols, width = inputs.shape[1:]
    local, size = blocks_gate.shape[:2]
    cw = cols // n
    seq_at, chan_at, dp_at = lax.axis_index("seq"), lax.axis_index("chan"), lax.axis_index("dp")
    core, x = lax.rem(dp_at, 2), dp_at // 2
    place = jnp.stack([seq_at, chan_at, core, x]).astype(jnp.int32)
    values, cot = inputs[0], cotangent[0]
    ahead, behind = mix_tables(cols_mix, seq_at, n, rows, cw)

    def relative(table):
        turned = jnp.roll(table, (local, local), (0, 1))
        table = jnp.where(chan_at == 0, table, turned).astype(F)
        return jnp.broadcast_to(table[:, :, None, :], table.shape[:2] + (8, size))

    ways = [
        lax.dynamic_slice_in_dim(values, lax.rem(seq_at + i, n) * cw, cw, 1) for i in range(n)
    ]
    x_cols = [ways[0]] + [shifted(ways[i], i, n) for i in range(1, n)]
    x_cols = [part.reshape(rows * cw, width) for part in x_cols]
    lent = pick(jnp.where(core == 0, blocks_gate, blocks_up), x)
    lent = swapped(lent, "chan", 1, 2)
    leaving, _ = lax.optimization_barrier((cot, lent))
    cot_oth = swapped(leaving, "chan", 1, 2)
    lent = [lent, swapped(lent, "dp", 2, 4)]
    mixes = (relative(mix_gate), relative(mix_up))

    x_cols, ahead, behind, mixes = lax.optimization_barrier((x_cols, ahead, behind, mixes))
    parts = column_mix(ahead, x_cols, n * rows, "column_mix")
    parts, lent = lax.optimization_barrier((parts, lent))
    passed = [swapped(block, "dp", 1, 4) for block in lent]
    parts = list(parts)
    held_up = [i for i in range(n * rows) if i not in (0, rows, 2 * rows)]
    late, passed = lax.optimization_barrier(([parts[i] for i in held_up], passed))
    for i, part in zip(held_up, late):
        parts[i] = part
    lent = lent + passed
    got = [
        [parts[h]] + [shifted(parts[i * rows + h], i, n) for i in range(1, n)]
        for h in range(rows)
    ]
    got[0], cot_oth = lax.optimization_barrier((got[0], cot_oth))
    hidden, mixed = [], []
    for h in range(rows):
        for held, value in zip((hidden, mixed), hidden_row(place, rows_in, values, h, got[h])):
            held.append(value)
    weights = (blocks_gate, blocks_up, *lent)
    others = [swapped(hidden[0], "chan", 1, 2)]
    for hid in hidden[1:]:
        hid, others[-1] = lax.optimization_barrier((hid, others[-1]))
        others.append(swapped(hid, "chan", 1, 2))
    others[0], hidden[-1] = lax.optimization_barrier((others[0], hidden[-1]))
    grads, back_g, back_u, pieces, mix_sum, rows_sum = [], [], [], [], [], []
    for h in range(rows):
        got = channel_row(
            place,
            h,
            hidden[h],
            others[h],
            cot,
            cot_oth,
            weights,
            mixes,
            rows_in,
            mixed[h],
            rows_sum,
        )
        for held, value in zip((grads, back_g, back_u, pieces, mix_sum), got):
            held.append(value)
        rows_sum = got[5:]
    kept, sent = sums(place, 4 * n, rows_sum[0], hidden, back_g, back_u, mix_sum)
    pieces[0], _ = lax.optimization_barrier((pieces[0], others[-1]))
    pieces[0] = traded(pieces[0].reshape(n, cw, width)).reshape(cols, width)
    sent, _ = lax.optimization_barrier((sent, pieces[0]))
    pieces[1], _ = lax.optimization_barrier((pieces[1], kept))
    pieces[1] = traded(pieces[1].reshape(n, cw, width)).reshape(cols, width)
    *leaving, fours = core_add(n, place, kept, swapped(sent, "dp", 1, 4))
    by_x = [swapped(shard, "dp", 2, 4) for shard in leaving]
    pieces[1], _ = lax.optimization_barrier((pieces[1], by_x[1]))
    turned = column_mix(behind, pieces, rows, "column_back")
    backs = [traded(turned[0].reshape(n, cw, width))]
    late, _ = lax.optimization_barrier((pieces[1], turned[0]))
    cols_sum = column_sum(cw, x_cols, [pieces[0], late])
    cols_sum = cols_sum.reshape(rows, n, n * rows, cw).sum(-1).transpose(1, 0, 2)
    cols_sum = turned_blocks(cols_sum.reshape(n * rows, n * rows), seq_at, -1, n, rows, 1)
    mine = scatter_seq(by_x, fours, cols_sum, n)
    held = [mine] + [shifted(mine, i, n) for i in range(1, n)]
    for part in turned[1:]:
        part, _ = lax.optimization_barrier((part, held[1]))
        backs.append(traded(part.reshape(n, cw, width)))
    backs = [part.reshape(cols, width) for part in backs]
    batch_all = lax.axis_size("dp")
    width_all = width * lax.axis_size("chan")
    rows_scale = 1.0 / math.sqrt(batch_all * rows * n * width_all)
    cols_scale = 1.0 / math.sqrt(batch_all * cols * width_all)
    block_scale = 1.0 / math.sqrt(batch_all * rows * n * cols)
    by_x = jnp.stack([swapped(shard, "dp", 2, 4) for shard in held])
    held = jnp.stack(held)
    by_core = swapped(held, "dp", 1, 4)
    done = []
    for h in range(rows):
        done = [finish(h, rows, grads[h], backs[h], done)]
    input_grad = done[0]
    gate_sum, up_sum, rows_sum, mix_g, mix_u, cols_sum = unpack(
        n,
        rows,
        local,
        (rows_scale, block_scale, cols_scale),
        place,
        (held, by_x, by_core, swapped(by_x, "dp", 1, 4)),
        cols,
    )
    return (
        input_grad[None],
        rows_sum,
        cols_sum,
        gate_sum.reshape(local, size, size),
        up_sum.reshape(local, size, size),
        mix_g,
        mix_u,
    )


def column_keep(segment, cols_mix):
    mixed = jnp.einsum(
        "er,brcd->becd", cols_mix, segment, preferred_element_type=jnp.float32
    ).astype(jnp.bfloat16)
    return (segment, mixed)

def body(inputs, cotangent, rows_in, cols_mix, blocks_gate, blocks_up, mix_gate, mix_up):
    batch_dev, rows_dev, cols_all, width_dev = inputs.shape
    block_size = blocks_gate.shape[1]
    local_blocks = blocks_gate.shape[0]
    chan_index = lax.axis_index("chan")
    split_shape = (batch_dev, rows_dev, cols_all, local_blocks, block_size)
    first = jnp.einsum("ec,brcd->bred", rows_in, inputs, preferred_element_type=jnp.float32).astype(
        jnp.bfloat16
    )
    first_cols, second_cols = column_keep(
        lax.all_to_all(first, "seq", split_axis=2, concat_axis=1, tiled=True), cols_mix
    )
    second_rows = lax.all_to_all(second_cols, "seq", split_axis=1, concat_axis=2, tiled=True)
    hidden = (inputs.astype(jnp.float32) + second_rows.astype(jnp.float32)).astype(jnp.bfloat16)
    hidden_blocks = hidden.reshape(split_shape)
    gate_rows_own = lax.dynamic_slice_in_dim(
        mix_gate, chan_index * local_blocks, local_blocks, 0
    ).astype(jnp.float32)
    up_rows_own = lax.dynamic_slice_in_dim(
        mix_up, chan_index * local_blocks, local_blocks, 0
    ).astype(jnp.float32)
    gate_mid = jnp.einsum(
        "brckj,kjl->brckl", hidden_blocks, blocks_gate, preferred_element_type=jnp.float32
    ).astype(jnp.bfloat16)
    up_mid = jnp.einsum(
        "brckj,kjl->brckl", hidden_blocks, blocks_up, preferred_element_type=jnp.float32
    ).astype(jnp.bfloat16)
    gate_add = jnp.einsum(
        "mkj,brckj->brcmj",
        gate_rows_own,
        lax.all_gather(gate_mid, "chan", axis=3, tiled=True).astype(jnp.float32),
    )
    up_add = jnp.einsum(
        "mkj,brckj->brcmj",
        up_rows_own,
        lax.all_gather(up_mid, "chan", axis=3, tiled=True).astype(jnp.float32),
    )
    upstream = cotangent.astype(jnp.float32).reshape(split_shape)
    sigma = jax.nn.sigmoid(gate_add)
    up_grad = (upstream * gate_add * sigma).astype(jnp.bfloat16)
    gate_grad = (upstream * up_add * sigma * (1.0 + gate_add * (1.0 - sigma))).astype(jnp.bfloat16)
    gate_all, up_all = (
        lax.all_gather(gate_grad, "chan", axis=3, tiled=True),
        lax.all_gather(up_grad, "chan", axis=3, tiled=True),
    )
    gate_cols_own = lax.dynamic_slice_in_dim(
        mix_gate, chan_index * local_blocks, local_blocks, 1
    ).astype(jnp.float32)
    up_cols_own = lax.dynamic_slice_in_dim(
        mix_up, chan_index * local_blocks, local_blocks, 1
    ).astype(jnp.float32)
    mix_gate_sum = jnp.einsum(
        "brcmj,brckj->mkj", gate_all, gate_mid, preferred_element_type=jnp.float32
    )
    mix_up_sum = jnp.einsum("brcmj,brckj->mkj", up_all, up_mid, preferred_element_type=jnp.float32)
    gate_back = jnp.einsum("mkj,brcmj->brckj", gate_cols_own, gate_all.astype(jnp.float32)).astype(
        jnp.bfloat16
    )
    up_back = jnp.einsum("mkj,brcmj->brckj", up_cols_own, up_all.astype(jnp.float32)).astype(
        jnp.bfloat16
    )
    blocks_gate_sum = jnp.einsum(
        "brckj,brckl->kjl", hidden_blocks, gate_back, preferred_element_type=jnp.float32
    )
    blocks_up_sum = jnp.einsum(
        "brckj,brckl->kjl", hidden_blocks, up_back, preferred_element_type=jnp.float32
    )
    hidden_grad = (
        upstream
        + jnp.einsum("brckl,kjl->brckj", gate_back, blocks_gate, preferred_element_type=jnp.float32)
        + jnp.einsum("brckl,kjl->brckj", up_back, blocks_up, preferred_element_type=jnp.float32)
    )
    hidden_grad = hidden_grad.reshape(inputs.shape).astype(jnp.bfloat16)
    segment = lax.all_to_all(hidden_grad, "seq", split_axis=2, concat_axis=1, tiled=True)
    mixed = jnp.einsum(
        "er,becd->brcd", cols_mix, segment, preferred_element_type=jnp.float32
    ).astype(jnp.bfloat16)
    cols_sum = jnp.einsum("becd,brcd->er", segment, first_cols, preferred_element_type=jnp.float32)
    first_grad = lax.all_to_all(mixed, "seq", split_axis=1, concat_axis=2, tiled=True)
    rows_sum = jnp.einsum("bred,brcd->ec", first_grad, inputs, preferred_element_type=jnp.float32)
    input_grad = (
        hidden_grad.astype(jnp.float32)
        + jnp.einsum("ec,bred->brcd", rows_in, first_grad, preferred_element_type=jnp.float32)
    ).astype(jnp.bfloat16)
    rows_total, cols_total = lax.psum((rows_sum, cols_sum), ("dp", "seq", "chan"))
    gate_blocks_total, up_blocks_total, gate_mix_total, up_mix_total = lax.psum(
        (blocks_gate_sum, blocks_up_sum, mix_gate_sum, mix_up_sum), ("dp", "seq")
    )
    count_dp = lax.axis_size("dp")
    count_seq = lax.axis_size("seq")
    count_chan = lax.axis_size("chan")
    batch_all = batch_dev * count_dp
    rows_all = rows_dev * count_seq
    width_all = width_dev * count_chan
    rows_scale = 1.0 / math.sqrt(batch_all * rows_all * width_all)
    cols_scale = 1.0 / math.sqrt(batch_all * cols_all * width_all)
    block_scale = 1.0 / math.sqrt(batch_all * rows_all * cols_all)
    return (
        input_grad,
        rows_total * rows_scale,
        cols_total * cols_scale,
        gate_blocks_total * block_scale,
        up_blocks_total * block_scale,
        gate_mix_total * block_scale,
        up_mix_total * block_scale,
    )


def solution(mesh):
    in_specs = (
        P("dp", "seq", None, "chan"),
        P("dp", "seq", None, "chan"),
        P(),
        P(),
        P("chan", None, None),
        P("chan", None, None),
        P(),
        P(),
    )
    out_specs = (
        P("dp", "seq", None, "chan"),
        P(),
        P(),
        P("chan", None, None),
        P("chan", None, None),
        P(None, "chan", None),
        P(None, "chan", None),
    )
    sizes = dict(mesh.shape)
    fits = sizes["dp"] == 4 and sizes["seq"] == 4 and sizes["chan"] == 2
    return jax.shard_map(block_body if fits else body, mesh=mesh, in_specs=in_specs, out_specs=out_specs, check_vma=False)
```
